32 devices in a mesh: facet: 8 (over y, x, core), dp: 4 (over z).
Axes of the slice: x: 2, y: 2, z: 4, core: 2. Of those that a mesh axis runs over, the one named last changes fastest.
Arguments:
- sky_image: float32 [64, 512, 256], P('dp', 'facet'), as said below
- wave_dual: float32 [64, 512, 256], P('dp', 'facet'), may hold values from -3 to 3
- rank_dual: float32 [64, 512, 256], P('dp', 'facet'), may hold values from -3 to 3
- data_dual: float32 [8, 8, 1024, 256], P('facet', 'dp'), may hold values from -3 to 3
- observed: bfloat16 [8, 8, 1024, 256], P('facet', 'dp'), may hold values from -6 to 6
- radius: float32 [8, 8, 256], P('facet', 'dp'), may hold values from 20 to 400
- degrid: bfloat16 [8, 8, 24, 1024, 128], P('facet', 'dp'), may hold values from -0.15625 to 0.15625
- tile_list: int32 [8, 8, 24], P(None, 'dp'), may hold values from 0 to 63, as said below
- counts: int32 [8, 8], P(None, 'dp'), may hold values from 6 to 24
- keep_count: int32 [8], P('facet'), may hold values from 2 to 64
Outputs:
- sky_next: float32 [64, 512, 256], P('dp', 'facet')
- wave_next: float32 [64, 512, 256], P('dp', 'facet')
- rank_next: float32 [64, 512, 256], P('dp', 'facet')
- data_next: float32 [8, 8, 1024, 256], P('facet', 'dp')
The draws below stay inside these ranges and needn't reach their ends.
Inputs may be any that keep to these rules, and one draw needn't show every extreme that they name: `sky_image`: nonnegative. `tile_list`: A slot's value is f * 8 + t, tile t of source facet f in the block's band. Among the live slots of the 2 blocks of one device (facet g, band d) at most 6 name one source facet; in every band some source facet is named by exactly 6 live slots of every device of that band.
All inputs are finite; a program needn't handle non-finite values.
Results may differ from the reference program's by a relative error of at most 0.005.
Values may be sent and summed in bfloat16 or wider, within the bound.
No kernel may reach another device: no remote copies, remote signals or barrier semaphores. Data moves between devices by JAX's collectives and lax.ppermute only.
A program may use at most 128 MiB of HBM per device.

```python
import math
import jax
import jax.numpy as jnp
from jax import lax

L = 256
TR = 8
TC = 16
HB = 16
WB = 64
NB = 2
KMAX = 24
VIS2 = 1024
FACETS = 8
BANDBLOCKS = 8
ROWS = 64
COLS = 512
NT = 8
CAP = 6
N_DP = 4


def routing(key):
    key_count, key_spot, key_hot, key_perm, key_tile, key_fill = jax.random.split(jax.random.fold_in(key, 11), 6)
    counts = jax.random.randint(key_count, (FACETS, BANDBLOCKS), KMAX // 4, KMAX + 1)
    spot = jax.random.randint(key_spot, (), 0, FACETS * BANDBLOCKS)
    flat_index = jnp.arange(FACETS * BANDBLOCKS).reshape(FACETS, BANDBLOCKS)
    counts = jnp.where(flat_index == spot, KMAX, counts).astype(jnp.int32)
    band_count = BANDBLOCKS // NB
    hot_source = jax.random.randint(key_hot, (band_count,), 0, FACETS)
    slot_count = NB * KMAX
    is_live = (jnp.arange(KMAX)[None, None, :] < counts[:, :, None]).reshape(FACETS, band_count, slot_count)
    live_order = jnp.cumsum(is_live.astype(jnp.int32), axis=2) - 1
    others = (FACETS - 1) * CAP
    perm_keys = jax.random.split(key_perm, FACETS * band_count)
    perms = jax.vmap(lambda subkey: jax.random.permutation(subkey, others))(perm_keys).reshape(FACETS, band_count, others)
    later = jnp.clip(live_order - CAP, 0, others - 1)
    picked = jnp.take_along_axis(perms, later, axis=2)
    relative = picked // CAP
    hot_grid = hot_source[None, :, None]
    spread = relative + (relative >= hot_grid).astype(jnp.int32)
    source = jnp.where(live_order < CAP, hot_grid, spread)
    filler = jax.random.randint(key_fill, source.shape, 0, FACETS)
    source = jnp.where(is_live, source, filler)
    local_tile = jax.random.randint(key_tile, source.shape, 0, NT)
    tiles = (source * NT + local_tile).reshape(FACETS, BANDBLOCKS, KMAX).astype(jnp.int32)
    return (counts, tiles)


def draw_counts(key, part):
    return routing(key)[0]


def draw_tile_list(key, part):
    return routing(key)[1]


def draw_keep_count(key, part):
    key_base, key_low, key_high = jax.random.split(jax.random.fold_in(key, 5), 3)
    keep = jax.random.randint(key_base, (FACETS,), 2, L // 4 + 1)
    low_spot = jax.random.randint(key_low, (), 0, FACETS)
    high_spot = (low_spot + 1 + jax.random.randint(key_high, (), 0, FACETS - 1)) % FACETS
    index = jnp.arange(FACETS)
    keep = jnp.where(index == low_spot, 2, keep)
    keep = jnp.where(index == high_spot, L // 4, keep)
    return keep.astype(jnp.int32)


def draw_sky_image(key, part):
    key_pix, key_chan, key_grain = jax.random.split(jax.random.fold_in(key, 3), 3)
    row_pos = jnp.arange(ROWS, dtype=jnp.float32)
    rising = 1.0 + 2.0 * row_pos / max(ROWS - 1, 1)
    pixel_scale = jnp.exp(jax.random.uniform(key_pix, (ROWS, COLS), jnp.float32, 0.0, math.log(10.0)))
    grain = jax.random.uniform(key_grain, (ROWS, COLS, L), jnp.float32, 0.5, 1.5)
    channel_scale = jnp.exp(jax.random.uniform(key_chan, (L,), jnp.float32, 0.0, math.log(10.0)))
    return 0.05 * (pixel_scale * rising[:, None])[:, :, None] * channel_scale[None, None, :] * grain


def levels(stream_key, shape, cuts, low, high):
    def one(position, parts):
        draws = jax.random.uniform(jax.random.fold_in(jax.random.fold_in(stream_key, 6), position), (parts,), jnp.float32, low / len(cuts), high / len(cuts))
        return jnp.repeat(jnp.exp(draws), shape[position] // parts).reshape((-1,) + (1,) * (len(shape) - position - 1))

    loudness = one(*cuts[0])
    for cut in cuts[1:]:
        loudness = loudness * one(*cut)
    return loudness


def gaussian(own_key, shape, scale, reach, cuts=(), held_as=jnp.bfloat16):
    level = levels(own_key, shape, cuts, -0.22, 0.18) if cuts else 1.0
    drawn = jax.random.normal(own_key, shape, jnp.float32) * scale * level
    return jnp.minimum(jnp.maximum(drawn, -reach), reach).astype(held_as)


def setup_inputs(seed: int = 0) -> dict:
    key_list = jax.random.split(jax.random.key(seed), 11)
    sky_image = draw_sky_image(jax.random.fold_in(key_list[10], 71), 0)
    wave_dual = gaussian(key_list[1], (ROWS, COLS, L), 0.5, 3.0, ((0, 4), (1, 8)), jnp.float32)
    rank_dual = gaussian(key_list[2], (ROWS, COLS, L), 0.5, 3.0, ((0, 4), (1, 8)), jnp.float32)
    data_dual = gaussian(key_list[3], (FACETS, BANDBLOCKS, VIS2, L), 0.5, 3.0, ((0, 8), (1, 4)), jnp.float32)
    observed = gaussian(key_list[4], (FACETS, BANDBLOCKS, VIS2, L), 1.0, 6.0, ((0, 8), (1, 4)))
    radius = jnp.clip(jnp.exp(math.log(400.0) - 2.9957323 * jax.random.uniform(key_list[5], (FACETS, BANDBLOCKS, L), jnp.float32) ** levels(key_list[5], (FACETS, BANDBLOCKS, L), ((0, 8), (1, 4)), -0.2, 0.2)), 20.0, 400.0)
    degrid = gaussian(key_list[6], (FACETS, BANDBLOCKS, KMAX, VIS2, TR * TC), (TR * TC * KMAX // 2) ** -0.5, 0.15625, ((0, 8), (1, 4)))
    tile_list = draw_tile_list(jax.random.fold_in(key_list[10], 71), 0)
    counts = draw_counts(jax.random.fold_in(key_list[10], 71), 0)
    keep_count = draw_keep_count(jax.random.fold_in(key_list[10], 71), 0)
    return {"sky_image": sky_image, "wave_dual": wave_dual, "rank_dual": rank_dual, "data_dual": data_dual, "observed": observed, "radius": radius, "degrid": degrid, "tile_list": tile_list, "counts": counts, "keep_count": keep_count}


wavelet_taps = (-0.12940952255126037, -0.2241438680420134, 0.8365163037378079, -0.48296291314453416)
step_primal = 0.5
step_wave = 0.5
wave_bound = 1.0
step_rank = 0.5

def analysis(padded, height, columns):
    across = sum((wavelet_taps[offset] * padded[offset + 1:offset + 1 + height, :, :] for offset in range(4)))
    return sum((wavelet_taps[offset] * across[:, offset + 1:offset + 1 + columns, :] for offset in range(4)))

def synthesis(padded, height, columns):
    across = sum((wavelet_taps[offset] * padded[3 - offset:3 - offset + height, :, :] for offset in range(4)))
    return sum((wavelet_taps[offset] * across[:, 3 - offset:3 - offset + columns, :] for offset in range(4)))

def to_band_tiles(field):
    shaped = field.reshape(N_DP, HB // TR, TR, FACETS, WB // TC, TC, L)
    return shaped.transpose(0, 3, 1, 4, 2, 5, 6).reshape(N_DP, FACETS * NT, TR * TC, L)

def from_band_tiles(tiles):
    shaped = tiles.reshape(N_DP, FACETS, HB // TR, WB // TC, TR, TC, L)
    return shaped.transpose(0, 2, 4, 1, 3, 5, 6).reshape(ROWS, COLS, L)

def reference(sky_image, wave_dual, rank_dual, data_dual, observed, radius, degrid, tile_list, counts, keep_count):
    workers = FACETS * BANDBLOCKS
    is_live = jnp.arange(KMAX, dtype=jnp.int32)[None, None, :] < counts[:, :, None]
    flat_degrid = degrid.reshape(workers, KMAX, VIS2, TR * TC)
    dual_half = data_dual.astype(jnp.bfloat16).reshape(workers, VIS2, L)
    flat_tiles = tile_list.reshape(workers, KMAX).astype(jnp.int32)
    flat_live = is_live.reshape(workers, KMAX)
    band_of = jnp.arange(workers, dtype=jnp.int32) % BANDBLOCKS // NB

    def adjoint_step(back_band, inputs):
        weights, dual_rows, tiles, live_mask, band = inputs
        contrib = jnp.einsum('kvp,vl->kpl', weights.astype(jnp.float32), dual_rows.astype(jnp.float32)).astype(jnp.bfloat16)
        contrib = jnp.where(live_mask[:, None, None], contrib.astype(jnp.float32), jnp.float32(0.0))
        return (back_band.at[band, tiles].add(contrib), None)
    start_band = jnp.zeros((N_DP, FACETS * NT, TR * TC, L), jnp.float32)
    back_band, unused_out = lax.scan(adjoint_step, start_band, (flat_degrid, dual_half, flat_tiles, flat_live, band_of))
    back = from_band_tiles(back_band)
    wave_pad = jnp.pad(wave_dual, ((2, 2), (2, 2), (0, 0)))
    gradient = back + synthesis(wave_pad, ROWS, COLS) + rank_dual
    sky_next = jnp.maximum(sky_image - step_primal * gradient, 0.0)
    extrap = 2.0 * sky_next - sky_image
    bar_pad = jnp.pad(extrap, ((2, 2), (2, 2), (0, 0)))
    wave_next = jnp.clip(wave_dual + step_wave * analysis(bar_pad, ROWS, COLS), -wave_bound, wave_bound)
    mixed = rank_dual + step_rank * extrap
    facet_view = mixed.reshape(ROWS, FACETS, WB, L).transpose(1, 0, 2, 3).reshape(FACETS, ROWS * WB, L)

    def rank_facet(inputs):
        view, kept = inputs
        gram = jnp.dot(view.T.astype(jnp.float32), view.astype(jnp.float32), precision=lax.Precision.HIGHEST, preferred_element_type=jnp.float32)
        level = (jnp.trace(gram) + 1e-06) / kept.astype(jnp.float32)
        factor = jnp.linalg.cholesky(gram + level * jnp.eye(L, dtype=jnp.float32))
        solved = jax.scipy.linalg.cho_solve((factor, True), view.T)
        return level * solved.T
    rank_view = lax.map(rank_facet, (facet_view, keep_count))
    rank_next = rank_view.reshape(FACETS, ROWS, WB, L).transpose(1, 0, 2, 3).reshape(ROWS, COLS, L)
    bar_tiles = to_band_tiles(extrap.astype(jnp.bfloat16))

    def forward_one(inputs):
        weights, tiles, live_mask, band = inputs
        chosen = bar_tiles[band, tiles]
        chosen = jnp.where(live_mask[:, None, None], chosen, jnp.zeros_like(chosen))
        return jnp.einsum('kvp,kpl->vl', weights.astype(jnp.float32), chosen.astype(jnp.float32))
    model = lax.map(forward_one, (flat_degrid, flat_tiles, flat_live, band_of)).reshape(FACETS, BANDBLOCKS, VIS2, L)
    misfit = data_dual + model - observed.astype(jnp.float32)
    size_norm = jnp.sqrt(lax.optimization_barrier(jnp.sum(misfit * misfit, axis=2)) + 1e-06)
    data_next = misfit * jnp.maximum(0.0, 1.0 - radius / size_norm)[:, :, None, :]
    return (sky_next, wave_next, rank_next, data_next)
```

```python
import functools

import jax
import jax.numpy as jnp
from jax import lax
from jax.experimental import pallas as pl
from jax.experimental.pallas import tpu as pltpu
from jax.sharding import PartitionSpec as P

TR = 8
TC = 16
MIB = 1 << 20


wavelet_taps = (-0.12940952255126037, -0.2241438680420134, 0.8365163037378079, -0.48296291314453416)
step_primal = 0.5
step_wave = 0.5
wave_bound = 1.0
step_rank = 0.5

any_spec = pl.BlockSpec(memory_space=pl.ANY)
smem_spec = pl.BlockSpec(memory_space=pltpu.SMEM)
vmem_spec = pl.BlockSpec(memory_space=pltpu.VMEM)


def padded_2(block, sides, width):
    for axis, dim in sides:
        count = lax.axis_size(axis)
        forward = [(i, i + 1) for i in range(count - 1)]
        backward = [(target, source) for source, target in forward]
        low = lax.ppermute(
            lax.slice_in_dim(block, block.shape[dim] - width, None, axis=dim), axis, forward
        )
        high = lax.ppermute(lax.slice_in_dim(block, 0, width, axis=dim), axis, backward)
        block = jnp.concatenate([low, block, high], axis=dim)
    return block


def analysis(padded, height, columns):
    across = sum(
        (
            wavelet_taps[offset] * padded[offset + 1 : offset + 1 + height, :, :]
            for offset in range(4)
        )
    )
    return sum(
        (
            wavelet_taps[offset] * across[:, offset + 1 : offset + 1 + columns, :]
            for offset in range(4)
        )
    )


def synthesis(padded, height, columns):
    across = sum(
        (
            wavelet_taps[offset] * padded[3 - offset : 3 - offset + height, :, :]
            for offset in range(4)
        )
    )
    return sum(
        (
            wavelet_taps[offset] * across[:, 3 - offset : 3 - offset + columns, :]
            for offset in range(4)
        )
    )


def swap(value, axis, mask):
    count = lax.axis_size(axis)
    return lax.ppermute(value, axis, [(i, i ^ mask) for i in range(count)])


def list_pairs(tiles_ref, counts_ref, slots, names, me, blocks, depth, tile_count, chips, far, dummy):
    total = jnp.int32(0)
    for b in range(blocks):
        count = counts_ref[me, b]

        def add(s, n, b=b, count=count):
            tile = tiles_ref[me, b, s]
            source = lax.div(tile, tile_count)
            relative = lax.bitwise_xor(source, me)
            is_far = lax.shift_right_logical(relative, 1) == chips - 1
            slots[n] = b * depth + s
            names[n] = relative * tile_count + (tile - source * tile_count)
            return n + jnp.where((s < count) & (is_far == far), 1, 0)

        begin = total
        total = lax.fori_loop(0, depth, add, total)
        odd = lax.rem(total - begin, 2)

        @pl.when(odd == 1)
        def _(total=total):
            slots[total] = slots[total - 1]
            names[total] = jnp.int32(dummy)

        total = total + odd
    return lax.div(total, 2)


def fetch_pair(degrid_hbm, slots, buf, sems, pair, depth, pixels, ring):
    copies = []
    place = lax.rem(pair, ring)
    for half in range(2):
        slot = slots[2 * pair + half]
        block = lax.div(slot, depth)
        copies.append(
            pltpu.make_async_copy(
                degrid_hbm.at[0, block, slot - block * depth],
                buf.at[place, :, pl.ds(half * pixels, pixels)],
                sems.at[place, half],
            )
        )
    return copies


def adjoint_body(
    tiles_ref, counts_ref, dual_ref, degrid_hbm, *refs, far, chips, tile_count, ring
):
    if far:
        even_ref, odd_ref, turned, acc, buf, sems, slots, names = refs
    else:
        even_ref, odd_ref, acc, buf, sems, slots, names = refs
        turned = dual_ref
    blocks, depth = degrid_hbm.shape[1:3]
    pixels = degrid_hbm.shape[4]
    me = lax.axis_index("facet")
    first = 2 * (chips - 1) * tile_count if far else 0
    live = acc.shape[0] - 1
    pairs = list_pairs(
        tiles_ref, counts_ref, slots, names, me, blocks, depth, tile_count, chips, far, first + live
    )
    for step in range(ring):
        @pl.when(step < pairs)
        def _():
            for copy in fetch_pair(degrid_hbm, slots, buf, sems, jnp.int32(step), depth, pixels, ring):
                copy.start()
    if far:
        for b in range(blocks):
            turned[b] = dual_ref[0, b].astype(jnp.bfloat16).T
    acc[...] = jnp.zeros_like(acc)

    def one(pair, carry):
        for copy in fetch_pair(degrid_hbm, slots, buf, sems, pair, depth, pixels, ring):
            copy.wait()
        block = lax.div(slots[2 * pair], depth)
        result = jnp.dot(
            turned[block], buf[lax.rem(pair, ring)], preferred_element_type=jnp.float32
        )
        result = result.astype(jnp.bfloat16).astype(jnp.float32)
        for half in range(2):
            place = names[2 * pair + half] - first
            acc[place] = acc[place] + result[:, half * pixels : (half + 1) * pixels]

        @pl.when(pair + ring < pairs)
        def _():
            for copy in fetch_pair(degrid_hbm, slots, buf, sems, pair + ring, depth, pixels, ring):
                copy.start()

        return carry

    lax.fori_loop(0, pairs, one, 0)
    for k in range(live // (2 * tile_count)):
        even_ref[k] = acc[2 * k * tile_count : (2 * k + 1) * tile_count].astype(jnp.bfloat16)
        odd_ref[k] = acc[(2 * k + 1) * tile_count : (2 * k + 2) * tile_count].astype(jnp.bfloat16)


def adjoint(tile_list, counts, dual, degrid, far, chips, tile_count):
    unused, blocks, depth, entries, pixels = degrid.shape
    channels = dual.shape[-1] if far else dual.shape[1]
    ring = 4
    share = 1 if far else chips - 1
    part = jax.ShapeDtypeStruct((share, tile_count, channels, pixels), jnp.bfloat16)
    out_shape = [part, part]
    if far:
        out_shape.append(jax.ShapeDtypeStruct((blocks, channels, entries), jnp.bfloat16))
    return pl.pallas_call(
        functools.partial(
            adjoint_body, far=far, chips=chips, tile_count=tile_count, ring=ring
        ),
        out_shape=out_shape,
        in_specs=[smem_spec, smem_spec, vmem_spec, any_spec],
        out_specs=[vmem_spec] * len(out_shape),
        scratch_shapes=[
            pltpu.VMEM((2 * share * tile_count + 1, channels, pixels), jnp.float32),
            pltpu.VMEM((ring, entries, 2 * pixels), jnp.bfloat16),
            pltpu.SemaphoreType.DMA((ring, 2)),
            pltpu.SMEM((blocks * (depth + 1),), jnp.int32),
            pltpu.SMEM((blocks * (depth + 1),), jnp.int32),
        ],
        compiler_params=pltpu.CompilerParams(vmem_limit_bytes=40 * MIB),
        name="adjoint_far" if far else "adjoint_near",
    )(tile_list, counts, dual, degrid)


def primal_body(*refs, parts):
    sky_ref, rest_ref, own_ref, mate_ref = refs[:4]
    halves = (refs[4 : 4 + parts], refs[4 + parts : 4 + 2 * parts])
    next_ref, extrap_ref = refs[4 + 2 * parts : 6 + 2 * parts]
    tile_refs = refs[6 + 2 * parts :]
    height, columns, channels = sky_ref.shape
    across = columns // TC
    for h in range(2):
        for t in range(tile_refs[h].shape[0]):
            tile = h * tile_refs[h].shape[0] + t
            total = own_ref[0, tile].astype(jnp.float32) + mate_ref[0, tile].astype(jnp.float32)
            for part in halves[h]:
                total = total + part[t].astype(jnp.float32)
            back = total.T.reshape(TR, TC, channels)
            rows = pl.ds(tile // across * TR, TR)
            cols = pl.ds(tile % across * TC, TC)
            sky = sky_ref[rows, cols, :]
            new = jnp.maximum(sky - step_primal * (back + rest_ref[rows, cols, :]), 0.0)
            extrap = 2.0 * new - sky
            next_ref[rows, cols, :] = new
            extrap_ref[rows, cols, :] = extrap
            tile_refs[h][t] = extrap.reshape(TR * TC, channels).astype(jnp.bfloat16)


def primal(sky, rest, own, mate, low, high):
    whole = jax.ShapeDtypeStruct(sky.shape, jnp.float32)
    half = jax.ShapeDtypeStruct(
        (own.shape[1] // 2, own.shape[3], own.shape[2]), jnp.bfloat16
    )
    lead = pl.BlockSpec((1,) + own.shape[1:], lambda i: (0, 0, 0, 0))
    return pl.pallas_call(
        functools.partial(primal_body, parts=len(low)),
        grid=(1,),
        out_shape=[whole, whole, half, half],
        in_specs=[vmem_spec, vmem_spec, lead, lead] + [vmem_spec] * (len(low) + len(high)),
        out_specs=[vmem_spec] * 4,
        compiler_params=pltpu.CompilerParams(vmem_limit_bytes=24 * MIB),
        name="primal",
    )(sky, rest, own, mate, *low, *high)


def gram_body(extrap_ref, rank_ref, packed_ref):
    height, columns, channels = extrap_ref.shape
    half = channels // 2
    mixed = (rank_ref[...] + step_rank * extrap_ref[...]).reshape(height * columns, channels)
    gram = lax.dot_general(
        mixed, mixed, (((0,), (0,)), ((), ())),
        precision=lax.Precision.HIGHEST, preferred_element_type=jnp.float32,
    )
    row = lax.broadcasted_iota(jnp.int32, (half, half), 0)
    col = lax.broadcasted_iota(jnp.int32, (half, half), 1)
    corner = gram[half:, half:]
    packed_ref[0:half] = jnp.where(col >= row, gram[:half, :half], corner)
    packed_ref[half:channels] = gram[:half, half:]
    packed_ref[channels:] = jnp.broadcast_to(
        jnp.sum(jnp.where(col == row, corner, 0.0), axis=0, keepdims=True), (8, half)
    )


def gram_of(extrap, rank_dual):
    channels = extrap.shape[2]
    return pl.pallas_call(
        gram_body,
        out_shape=jax.ShapeDtypeStruct((channels + 8, channels // 2), jnp.float32),
        in_specs=[vmem_spec, vmem_spec],
        out_specs=vmem_spec,
        compiler_params=pltpu.CompilerParams(vmem_limit_bytes=24 * MIB),
        name="gram",
    )(extrap, rank_dual)


def split(value):
    high = value.astype(jnp.bfloat16)
    return high, (value - high.astype(jnp.float32)).astype(jnp.bfloat16)


def dot_fine(left, right):
    a, b = split(left)
    c, d = split(right)
    return (
        jnp.dot(a, c, preferred_element_type=jnp.float32)
        + jnp.dot(a, d, preferred_element_type=jnp.float32)
        + jnp.dot(b, c, preferred_element_type=jnp.float32)
    )


def dot_full(left, right):
    return jnp.dot(
        left, right, precision=lax.Precision.HIGHEST, preferred_element_type=jnp.float32
    )


def dot_quick(left, right):
    return jnp.dot(
        left.astype(jnp.bfloat16), right.astype(jnp.bfloat16), preferred_element_type=jnp.float32
    )


def rank_body(keep_ref, *refs, parts):
    packed_refs = refs[:parts]
    extrap_hbm, rank_hbm, out_ref, extrap_buf, rank_buf, sems = refs[parts:]
    loads = [
        pltpu.make_async_copy(extrap_hbm, extrap_buf, sems.at[0]),
        pltpu.make_async_copy(rank_hbm, rank_buf, sems.at[1]),
    ]
    for load in loads:
        load.start()
    height, columns, channels = extrap_buf.shape
    half = channels // 2
    packed = packed_refs[0][...]
    for ref in packed_refs[1:]:
        packed = packed + ref[...]
    row = lax.broadcasted_iota(jnp.int32, (half, half), 0)
    col = lax.broadcasted_iota(jnp.int32, (half, half), 1)
    mix = packed[:half]
    upper = jnp.where(col > row, mix, 0.0)
    lower = jnp.where(col < row, mix, 0.0)
    first = jnp.where(col >= row, mix, 0.0) + upper.T
    tail = packed[channels : channels + 1]
    last = lower + lower.T + jnp.where(col == row, jnp.broadcast_to(tail, (half, half)), 0.0)
    cross = packed[half:channels]
    gram = jnp.concatenate(
        [jnp.concatenate([first, cross], axis=1), jnp.concatenate([cross.T, last], axis=1)], axis=0
    )
    wide_row = lax.broadcasted_iota(jnp.int32, (channels, channels), 0)
    wide_col = lax.broadcasted_iota(jnp.int32, (channels, channels), 1)
    eye = jnp.where(wide_row == wide_col, 1.0, 0.0).astype(jnp.float32)
    keep = jnp.full((1, 1), keep_ref[0], jnp.int32).astype(jnp.float32)
    trace = jnp.sum(jnp.sum(gram * eye, axis=0, keepdims=True), axis=1, keepdims=True)
    level = (trace + 1e-06) / keep
    system = gram / level + eye
    scale = 2.0 / (2.0 + keep)
    inverse = scale * (2.0 * eye - scale * system)
    for _ in range(6):
        residual = eye - dot_quick(system, inverse)
        inverse = inverse + dot_quick(inverse, residual)
    for _ in range(2):
        residual = eye - dot_fine(system, inverse)
        inverse = inverse + dot_fine(inverse, residual)
    residual = eye - dot_full(system, inverse)
    inverse = inverse + dot_fine(inverse, residual)
    for load in loads:
        load.wait()
    mixed = (rank_buf[...] + step_rank * extrap_buf[...]).reshape(height * columns, channels)
    out_ref[...] = dot_fine(mixed, inverse).reshape(height, columns, channels)


def rank_update(keep_count, packed, extrap, rank_dual):
    return pl.pallas_call(
        functools.partial(rank_body, parts=len(packed)),
        out_shape=jax.ShapeDtypeStruct(extrap.shape, jnp.float32),
        in_specs=[smem_spec] + [vmem_spec] * len(packed) + [any_spec, any_spec],
        out_specs=vmem_spec,
        scratch_shapes=[
            pltpu.VMEM(extrap.shape, jnp.float32),
            pltpu.VMEM(extrap.shape, jnp.float32),
            pltpu.SemaphoreType.DMA((2,)),
        ],
        compiler_params=pltpu.CompilerParams(vmem_limit_bytes=32 * MIB),
        name="rank",
    )(keep_count, *packed, extrap, rank_dual)


def forward_body(tiles_ref, counts_ref, degrid_hbm, *refs, far, chips, tile_count, ring, held):
    image_hbm = refs[: 2 * held]
    if far:
        start_ref, radius_ref, out_ref = refs[2 * held : 2 * held + 3]
        rest = refs[2 * held + 3 :]
    else:
        dual_ref, seen_ref, out_ref = refs[2 * held : 2 * held + 3]
        rest = refs[2 * held + 3 :]
    image, acc, buf, sems, image_sems, slots, names = rest
    blocks, depth, entries, pixels = degrid_hbm.shape[1:5]
    me = lax.axis_index("facet")
    first = 2 * (chips - 1) * tile_count if far else 0
    live = held * tile_count
    loads = [
        pltpu.make_async_copy(
            image_hbm[i],
            image.at[pl.ds(i * tile_count // 2, tile_count // 2)],
            image_sems.at[i],
        )
        for i in range(2 * held)
    ]
    for load in loads:
        load.start()
    pairs = list_pairs(
        tiles_ref, counts_ref, slots, names, me, blocks, depth, tile_count, chips, far, first + live
    )
    for step in range(ring):
        @pl.when(step < pairs)
        def _():
            for copy in fetch_pair(degrid_hbm, slots, buf, sems, jnp.int32(step), depth, pixels, ring):
                copy.start()
    image[live] = jnp.zeros_like(image[live])
    for b in range(blocks):
        if far:
            acc[b] = start_ref[b]
        else:
            acc[b] = dual_ref[0, b] - seen_ref[0, b].astype(jnp.float32)
    for load in loads:
        load.wait()

    def one(pair, carry):
        for copy in fetch_pair(degrid_hbm, slots, buf, sems, pair, depth, pixels, ring):
            copy.wait()
        block = lax.div(slots[2 * pair], depth)
        right = jnp.concatenate(
            [image[names[2 * pair] - first], image[names[2 * pair + 1] - first]], axis=0
        )
        acc[block] = acc[block] + jnp.dot(
            buf[lax.rem(pair, ring)], right, preferred_element_type=jnp.float32
        )

        @pl.when(pair + ring < pairs)
        def _():
            for copy in fetch_pair(degrid_hbm, slots, buf, sems, pair + ring, depth, pixels, ring):
                copy.start()

        return carry

    lax.fori_loop(0, pairs, one, 0)
    for b in range(blocks):
        misfit = acc[b]
        if far:
            size = jnp.sqrt(jnp.sum(misfit * misfit, axis=0, keepdims=True) + 1e-06)
            scale = jnp.maximum(0.0, 1.0 - radius_ref[0, b : b + 1, :] / size)
            out_ref[0, b] = misfit * scale
        else:
            out_ref[b] = misfit


def forward(tile_list, counts, degrid, image, extra, far, chips, tile_count):
    unused, blocks, depth, entries, pixels = degrid.shape
    channels = image[0].shape[-1]
    ring = 4
    held = len(image) // 2
    out_shape = (1, blocks, entries, channels) if far else (blocks, entries, channels)
    return pl.pallas_call(
        functools.partial(
            forward_body, far=far, chips=chips, tile_count=tile_count, ring=ring, held=held
        ),
        out_shape=jax.ShapeDtypeStruct(out_shape, jnp.float32),
        in_specs=[smem_spec, smem_spec, any_spec]
        + [any_spec] * len(image)
        + [vmem_spec] * len(extra),
        out_specs=vmem_spec,
        scratch_shapes=[
            pltpu.VMEM((held * tile_count + 1, pixels, channels), jnp.bfloat16),
            pltpu.VMEM((blocks, entries, channels), jnp.float32),
            pltpu.VMEM((ring, entries, 2 * pixels), jnp.bfloat16),
            pltpu.SemaphoreType.DMA((ring, 2)),
            pltpu.SemaphoreType.DMA((2 * held,)),
            pltpu.SMEM((blocks * (depth + 1),), jnp.int32),
            pltpu.SMEM((blocks * (depth + 1),), jnp.int32),
        ],
        compiler_params=pltpu.CompilerParams(vmem_limit_bytes=40 * MIB),
        name="forward_far" if far else "forward_near",
    )(tile_list, counts, degrid, *image, *extra)


def plus(*values):
    total = values[0].astype(jnp.float32)
    for value in values[1:]:
        total = total + value.astype(jnp.float32)
    return total.astype(jnp.bfloat16)


def to_owners(even_far, odd_far, even_near, odd_near, chips):
    half = even_far.shape[1] // 2
    mate_far = swap(odd_far, "facet", 1)
    mate_near = swap(odd_near, "facet", 1)
    low, high = slice(0, half), slice(half, None)
    if chips == 4:
        to_x = plus(even_far[0, low], mate_far[0, low])
        to_y = plus(even_far[0, high], mate_far[0, high])
        via_x = swap(to_x, "facet", 2)
        via_y = swap(to_y, "facet", 4)
        x_low = swap(plus(even_near[1, low], mate_near[1, low]), "facet", 2)
        y_high = swap(plus(even_near[2, high], mate_near[2, high]), "facet", 4)
        x_high = swap(plus(even_near[1, high], mate_near[1, high], via_y), "facet", 2)
        y_low = swap(plus(even_near[2, low], mate_near[2, low], via_x), "facet", 4)
        return mate_near, [x_low, y_low], [x_high, y_high]
    lows, highs = [], []
    for k in range(1, chips):
        even, mate = (even_far[0], mate_far[0]) if k == chips - 1 else (even_near[k], mate_near[k])
        got = swap(plus(even, mate), "facet", 2 * k)
        lows.append(got[low])
        highs.append(got[high])
    return mate_near, lows, highs


def from_owners(low, high, chips):
    reached = {0: (low, high)}
    if chips == 4:
        x_low = swap(low, "facet", 2)
        y_high = swap(high, "facet", 4)
        x_high = swap(high, "facet", 2)
        y_low = swap(low, "facet", 4)
        reached[1] = (x_low, x_high)
        reached[2] = (y_low, y_high)
        reached[3] = (swap(x_low, "facet", 4), swap(y_high, "facet", 2))
    else:
        for k in range(1, chips):
            reached[k] = (swap(low, "facet", 2 * k), swap(high, "facet", 2 * k))
    image = []
    for k in range(chips):
        image.extend(reached[k])
        image.extend(swap(part, "facet", 1) for part in reached[k])
    return image


def per_device(
    sky_image,
    wave_dual,
    rank_dual,
    data_dual,
    observed,
    radius,
    degrid,
    tile_list,
    counts,
    keep_count,
):
    height, columns, channels = sky_image.shape
    facets = lax.axis_size("facet")
    chips = facets // 2
    tile_count = height // TR * (columns // TC)

    even_far, odd_far, turned = adjoint(
        tile_list, counts, data_dual, degrid, True, chips, tile_count
    )
    even_near, odd_near = adjoint(tile_list, counts, turned, degrid, False, chips, tile_count)
    mate_near, low, high = to_owners(even_far, odd_far, even_near, odd_near, chips)

    wave_halo = padded_2(wave_dual, (("facet", 1), ("dp", 0)), 2)
    rest = synthesis(wave_halo, height, columns) + rank_dual
    sky_next, extrap, tiles_low, tiles_high = primal(
        sky_image, rest, even_near, mate_near, low, high
    )

    image = from_owners(tiles_low, tiles_high, chips)
    packed = gram_of(extrap, rank_dual)
    everyone = [packed] + [swap(packed, "dp", k) for k in range(1, lax.axis_size("dp"))]
    bar_halo = padded_2(extrap, (("facet", 1), ("dp", 0)), 2)
    wave_next = jnp.clip(
        wave_dual + step_wave * analysis(bar_halo, height, columns), -wave_bound, wave_bound
    )
    cut = 4 * (chips - 1)
    near = forward(
        tile_list, counts, degrid, image[:cut], (data_dual, observed), False, chips, tile_count
    )
    rank_next = rank_update(keep_count, everyone, extrap, rank_dual)
    data_next = forward(
        tile_list, counts, degrid, image[cut:], (near, radius), True, chips, tile_count
    )
    return (sky_next, wave_next, rank_next, data_next)


def solution(mesh):
    return jax.shard_map(
        per_device,
        mesh=mesh,
        in_specs=(
            P("dp", "facet", None),
            P("dp", "facet", None),
            P("dp", "facet", None),
            P("facet", "dp", None, None),
            P("facet", "dp", None, None),
            P("facet", "dp", None),
            P("facet", "dp", None, None, None),
            P(None, "dp", None),
            P(None, "dp"),
            P("facet"),
        ),
        out_specs=(
            P("dp", "facet", None),
            P("dp", "facet", None),
            P("dp", "facet", None),
            P("facet", "dp", None, None),
        ),
        check_vma=False,
    )
```

```python
import functools

import jax
import jax.numpy as jnp
from jax import lax
from jax.experimental import pallas as pl
from jax.experimental.pallas import tpu as pltpu
from jax.sharding import PartitionSpec as P


TR = 8
TC = 16
MIB = 1 << 20


wavelet_taps = (-0.12940952255126037, -0.2241438680420134, 0.8365163037378079, -0.48296291314453416)
step_primal = 0.5
step_wave = 0.5
wave_bound = 1.0
step_rank = 0.5

any_spec = pl.BlockSpec(memory_space=pl.ANY)
smem_spec = pl.BlockSpec(memory_space=pltpu.SMEM)
hbm_spec = pl.BlockSpec(memory_space=pltpu.HBM)
vmem_spec = pl.BlockSpec(memory_space=pltpu.VMEM)
adjoint_group = 8
forward_group = 8


def in_hbm(value):
    return pltpu.with_memory_space_constraint(value, pltpu.HBM)


def swap(value, axis, mask):
    count = lax.axis_size(axis)
    return lax.ppermute(value, axis, [(i, i ^ mask) for i in range(count)])


def padded_2(block, sides, width):
    for axis, dim, even in sides:
        count = lax.axis_size(axis)
        outer = [(i, i + 1) for i in range(1, count - 1, 2)]
        outer = outer + [(target, source) for source, target in outer]
        first = lax.slice_in_dim(block, 0, width, axis=dim)
        last = lax.slice_in_dim(block, block.shape[dim] - width, None, axis=dim)
        inward = jnp.where(even, last, first)
        outward = jnp.where(even, first, last)
        inside = swap(inward, axis, 1)
        outside = lax.ppermute(outward, axis, outer)
        low = jnp.where(even, outside, inside)
        high = jnp.where(even, inside, outside)
        block = jnp.concatenate([low, block, high], axis=dim)
    return block


def analysis(padded, height, columns):
    across = sum(
        (
            wavelet_taps[offset] * padded[offset + 1 : offset + 1 + height, :, :]
            for offset in range(4)
        )
    )
    return sum(
        (
            wavelet_taps[offset] * across[:, offset + 1 : offset + 1 + columns, :]
            for offset in range(4)
        )
    )


def synthesis(padded, height, columns):
    across = sum(
        (
            wavelet_taps[offset] * padded[3 - offset : 3 - offset + height, :, :]
            for offset in range(4)
        )
    )
    return sum(
        (
            wavelet_taps[offset] * across[:, 3 - offset : 3 - offset + columns, :]
            for offset in range(4)
        )
    )


def slot_chunks(degrid_hbm, buf, sems, group):
    blocks, depth = degrid_hbm.shape[1:3]
    return [
        [
            pltpu.make_async_copy(
                degrid_hbm.at[0, b, pl.ds(c * group, group)],
                buf.at[b, pl.ds(c * group, group)],
                sems.at[b, c],
            )
            for c in range(depth // group)
        ]
        for b in range(blocks)
    ]


def relative_tile(tiles, me, block, slot, count, tile_count, dummy):
    tile = tiles[me, block, jnp.minimum(slot, count - 1)]
    source = lax.div(tile, tile_count)
    place = lax.bitwise_xor(source, me) * tile_count + (tile - source * tile_count)
    return jnp.where(slot < count, place, dummy)


def adjoint_body(
    tiles_hbm, counts_hbm, dual_hbm, degrid_hbm,
    even_far_ref, even_mid_ref, even_own_ref, odd_far_ref, odd_mid_ref, odd_own_ref,
    tiles, counts, dual, turned, acc, buf, sems, dual_sems, list_sems,
    *, chips, tile_count, group,
):
    blocks, depth = degrid_hbm.shape[1:3]
    pixels = degrid_hbm.shape[4]
    me = lax.axis_index("facet")
    chunks = slot_chunks(degrid_hbm, buf, sems, group)
    lists = [
        pltpu.make_async_copy(counts_hbm, counts, list_sems.at[0]),
        pltpu.make_async_copy(tiles_hbm, tiles, list_sems.at[1]),
    ]
    duals = [
        pltpu.make_async_copy(dual_hbm.at[0, b], dual.at[b], dual_sems.at[b]) for b in range(blocks)
    ]
    for copy in lists + duals:
        copy.start()
    for b in range(blocks):
        chunks[b][0].start()
    for copy in lists:
        copy.wait()
    for b in range(blocks):
        for c in range(1, depth // group):
            @pl.when(c * group < counts[b, me])
            def _():
                chunks[b][c].start()
    live = 2 * chips * tile_count
    acc[...] = jnp.zeros_like(acc)
    for b in range(blocks):
        duals[b].wait()
        turned[b] = dual[b].astype(jnp.bfloat16).T
    for b in range(blocks):
        for c in range(depth // group):
            @pl.when(c * group < counts[b, me])
            def _():
                chunks[b][c].wait()
                right = jnp.concatenate([buf[b, c * group + j] for j in range(group)], axis=1)
                result = jnp.dot(turned[b], right, preferred_element_type=jnp.float32)
                result = result.astype(jnp.bfloat16).astype(jnp.float32)
                for j in range(group):
                    name = relative_tile(
                        tiles, me, b, c * group + j, counts[b, me], tile_count, live
                    )
                    acc[name] = acc[name] + result[:, j * pixels : (j + 1) * pixels]

    for k in range(chips):
        first = 2 * k * tile_count
        even = acc[first : first + tile_count].astype(jnp.bfloat16)
        odd = acc[first + tile_count : first + 2 * tile_count].astype(jnp.bfloat16)
        if k == chips - 1:
            even_far_ref[...] = even
            odd_far_ref[...] = odd
        elif k:
            even_mid_ref[k - 1] = even
            odd_mid_ref[k - 1] = odd
        else:
            even_own_ref[...] = even
            odd_own_ref[...] = odd


def adjoint(tile_list, counts, dual, degrid, chips, tile_count):
    _, blocks, depth, entries, pixels = degrid.shape
    channels = dual.shape[-1]
    group = adjoint_group

    def tiles_of(*lead):
        return jax.ShapeDtypeStruct(lead + (tile_count, channels, pixels), jnp.bfloat16)

    return pl.pallas_call(
        functools.partial(adjoint_body, chips=chips, tile_count=tile_count, group=group),
        out_shape=[tiles_of(), tiles_of(chips - 2), tiles_of()] * 2,
        in_specs=[hbm_spec] * 4,
        out_specs=[vmem_spec] * 6,
        scratch_shapes=[
            pltpu.SMEM(tile_list.shape, jnp.int32),
            pltpu.SMEM(counts.shape, jnp.int32),
            pltpu.VMEM((blocks, entries, channels), jnp.float32),
            pltpu.VMEM((blocks, channels, entries), jnp.bfloat16),
            pltpu.VMEM((2 * chips * tile_count + 1, channels, pixels), jnp.float32),
            pltpu.VMEM((blocks, depth, entries, pixels), jnp.bfloat16),
            pltpu.SemaphoreType.DMA((blocks, depth // group)),
            pltpu.SemaphoreType.DMA((blocks,)),
            pltpu.SemaphoreType.DMA((2,)),
        ],
        compiler_params=pltpu.CompilerParams(vmem_limit_bytes=(30 if chips == 4 else 50) * MIB),
        name="adjoint",
    )(*(in_hbm(value) for value in (tile_list, counts, dual, degrid)))


def primal_body(*refs, parts):
    sky_ref, rest_ref, own_ref, mate_ref = refs[:4]
    halves = (refs[4 : 4 + parts], refs[4 + parts : 4 + 2 * parts])
    next_ref, extrap_ref = refs[4 + 2 * parts : 6 + 2 * parts]
    tiles_ref = refs[6 + 2 * parts]
    _, columns, channels = sky_ref.shape
    across = columns // TC
    half = tiles_ref.shape[0] // 2
    for h in range(2):
        for t in range(half):
            tile = h * half + t
            total = own_ref[tile].astype(jnp.float32) + mate_ref[tile].astype(jnp.float32)
            for part in halves[h]:
                total = total + part[t].astype(jnp.float32)
            back = total.T.reshape(TR, TC, channels)
            rows = pl.ds(tile // across * TR, TR)
            cols = pl.ds(tile % across * TC, TC)
            sky = sky_ref[rows, cols, :]
            new = jnp.maximum(sky - step_primal * (back + rest_ref[rows, cols, :]), 0.0)
            extrap = 2.0 * new - sky
            next_ref[rows, cols, :] = new
            extrap_ref[rows, cols, :] = extrap
            tiles_ref[tile] = extrap.reshape(TR * TC, channels).astype(jnp.bfloat16)


def primal(sky, rest, own, mate, low, high):
    whole = jax.ShapeDtypeStruct(sky.shape, jnp.float32)
    tiles = jax.ShapeDtypeStruct((own.shape[0], own.shape[2], own.shape[1]), jnp.bfloat16)
    return pl.pallas_call(
        functools.partial(primal_body, parts=len(low)),
        out_shape=[whole, whole, tiles],
        in_specs=[vmem_spec] * (4 + len(low) + len(high)),
        out_specs=[vmem_spec] * 3,
        compiler_params=pltpu.CompilerParams(vmem_limit_bytes=24 * MIB),
        name="primal",
    )(sky, rest, own, mate, *low, *high)


def gram_body(extrap_ref, rank_ref, packed_ref):
    height, columns, channels = extrap_ref.shape
    half = channels // 2
    mixed = (rank_ref[...] + step_rank * extrap_ref[...]).reshape(height * columns, channels)
    gram = lax.dot_general(
        mixed, mixed, (((0,), (0,)), ((), ())),
        precision=lax.Precision.HIGHEST, preferred_element_type=jnp.float32,
    )
    row = lax.broadcasted_iota(jnp.int32, (half, half), 0)
    col = lax.broadcasted_iota(jnp.int32, (half, half), 1)
    corner = gram[half:, half:]
    packed_ref[0:half] = jnp.where(col >= row, gram[:half, :half], corner)
    packed_ref[half:channels] = gram[:half, half:]
    packed_ref[channels:] = jnp.broadcast_to(
        jnp.sum(jnp.where(col == row, corner, 0.0), axis=0, keepdims=True), (8, half)
    )


def gram_of(extrap, rank_dual):
    channels = extrap.shape[2]
    return pl.pallas_call(
        gram_body,
        out_shape=jax.ShapeDtypeStruct((channels + 8, channels // 2), jnp.float32),
        in_specs=[vmem_spec, vmem_spec],
        out_specs=vmem_spec,
        compiler_params=pltpu.CompilerParams(vmem_limit_bytes=24 * MIB),
        name="gram",
    )(extrap, rank_dual)


def split(value):
    high = value.astype(jnp.bfloat16)
    return high, (value - high.astype(jnp.float32)).astype(jnp.bfloat16)


def dot_fine(left, right):
    a, b = split(left)
    c, d = split(right)
    return (
        jnp.dot(a, c, preferred_element_type=jnp.float32)
        + jnp.dot(a, d, preferred_element_type=jnp.float32)
        + jnp.dot(b, c, preferred_element_type=jnp.float32)
    )


def dot_full(left, right):
    return jnp.dot(
        left, right, precision=lax.Precision.HIGHEST, preferred_element_type=jnp.float32
    )


def dot_quick(left, right):
    return jnp.dot(
        left.astype(jnp.bfloat16), right.astype(jnp.bfloat16), preferred_element_type=jnp.float32
    )


def rank_body(keep_ref, *refs, parts):
    packed_refs = refs[:parts]
    extrap_hbm, rank_hbm, out_ref, extrap_buf, rank_buf, sems = refs[parts:]
    loads = [
        pltpu.make_async_copy(extrap_hbm, extrap_buf, sems.at[0]),
        pltpu.make_async_copy(rank_hbm, rank_buf, sems.at[1]),
    ]
    for load in loads:
        load.start()
    height, columns, channels = extrap_buf.shape
    half = channels // 2
    packed = packed_refs[0][...]
    for ref in packed_refs[1:]:
        packed = packed + ref[...]
    row = lax.broadcasted_iota(jnp.int32, (half, half), 0)
    col = lax.broadcasted_iota(jnp.int32, (half, half), 1)
    mix = packed[:half]
    upper = jnp.where(col > row, mix, 0.0)
    lower = jnp.where(col < row, mix, 0.0)
    first = jnp.where(col >= row, mix, 0.0) + upper.T
    tail = packed[channels : channels + 1]
    last = lower + lower.T + jnp.where(col == row, jnp.broadcast_to(tail, (half, half)), 0.0)
    cross = packed[half:channels]
    gram = jnp.concatenate(
        [jnp.concatenate([first, cross], axis=1), jnp.concatenate([cross.T, last], axis=1)], axis=0
    )
    wide_row = lax.broadcasted_iota(jnp.int32, (channels, channels), 0)
    wide_col = lax.broadcasted_iota(jnp.int32, (channels, channels), 1)
    eye = jnp.where(wide_row == wide_col, 1.0, 0.0).astype(jnp.float32)
    keep = jnp.full((1, 1), keep_ref[0], jnp.int32).astype(jnp.float32)
    trace = jnp.sum(jnp.sum(gram * eye, axis=0, keepdims=True), axis=1, keepdims=True)
    level = (trace + 1e-06) / keep
    system = gram / level + eye
    scale = 2.0 / (2.0 + keep)
    error = eye - scale * system
    inverse = scale * (eye + error)
    error = dot_quick(error, error)
    for step in range(6):
        if step < 5:
            both = dot_quick(jnp.concatenate([inverse, error], axis=0), error)
            inverse = inverse + both[:channels]
            error = both[channels:]
        else:
            inverse = inverse + dot_quick(inverse, error)
    for _ in range(2):
        residual = eye - dot_fine(system, inverse)
        inverse = inverse + dot_fine(inverse, residual)
    residual = eye - dot_full(system, inverse)
    inverse = inverse + dot_fine(inverse, residual)
    for load in loads:
        load.wait()
    mixed = (rank_buf[...] + step_rank * extrap_buf[...]).reshape(height * columns, channels)
    out_ref[...] = dot_fine(mixed, inverse).reshape(height, columns, channels)


def rank_update(keep_count, packed, extrap, rank_dual):
    return pl.pallas_call(
        functools.partial(rank_body, parts=len(packed)),
        out_shape=jax.ShapeDtypeStruct(extrap.shape, jnp.float32),
        in_specs=[smem_spec] + [vmem_spec] * len(packed) + [any_spec, any_spec],
        out_specs=vmem_spec,
        scratch_shapes=[
            pltpu.VMEM(extrap.shape, jnp.float32),
            pltpu.VMEM(extrap.shape, jnp.float32),
            pltpu.SemaphoreType.DMA((2,)),
        ],
        compiler_params=pltpu.CompilerParams(vmem_limit_bytes=32 * MIB),
        name="rank",
    )(keep_count, *packed, extrap, rank_dual)


def forward_body(
    tiles_hbm, counts_hbm, degrid_hbm, dual_hbm, seen_hbm, radius_ref, *refs,
    chips, tile_count, group,
):
    held = 2 * chips
    image_refs, out_hbm = refs[:held], refs[held]
    tiles, counts, dual, seen, image, acc, buf, sems, image_sems, wide_sems, list_sems = refs[
        held + 1 :
    ]
    blocks, depth, _, _ = degrid_hbm.shape[1:5]
    me = lax.axis_index("facet")
    chunks = slot_chunks(degrid_hbm, buf, sems, group)
    lists = [
        pltpu.make_async_copy(counts_hbm, counts, list_sems.at[0]),
        pltpu.make_async_copy(tiles_hbm, tiles, list_sems.at[1]),
    ]
    images = [
        pltpu.make_async_copy(
            image_refs[i], image.at[pl.ds(i * tile_count, tile_count)], image_sems.at[i]
        )
        for i in range(held)
    ]
    wide = [
        pltpu.make_async_copy(dual_hbm.at[0], dual, wide_sems.at[0]),
        pltpu.make_async_copy(seen_hbm.at[0], seen, wide_sems.at[1]),
    ]
    stores = [
        pltpu.make_async_copy(acc.at[b], out_hbm.at[0, b], wide_sems.at[2 + b]) for b in range(blocks)
    ]
    for copy in lists:
        copy.start()
    chunks[0][0].start()
    for copy in images:
        copy.start()
    for b in range(1, blocks):
        chunks[b][0].start()
    for copy in lists:
        copy.wait()
    for b in range(blocks):
        for c in range(1, depth // group):
            @pl.when(c * group < counts[b, me])
            def _():
                chunks[b][c].start()
        if b == 0:
            for copy in wide:
                copy.start()
    live = held * tile_count
    image[live] = jnp.zeros_like(image[live])
    for copy in images:
        copy.wait()
    for b in range(blocks):
        for c in range(depth // group):
            @pl.when(c * group < counts[b, me])
            def _():
                chunks[b][c].wait()
                names = [
                    relative_tile(tiles, me, b, c * group + j, counts[b, me], tile_count, live)
                    for j in range(group)
                ]
                left = jnp.concatenate([buf[b, c * group + j] for j in range(group)], axis=1)
                right = jnp.concatenate([image[name] for name in names], axis=0)
                product = jnp.dot(left, right, preferred_element_type=jnp.float32)
                acc[b] = acc[b] + product if c else product

        if b == 0:
            for copy in wide:
                copy.wait()
        misfit = acc[b] + (dual[b] - seen[b].astype(jnp.float32))
        size = jnp.sqrt(jnp.sum(misfit * misfit, axis=0, keepdims=True) + 1e-06)
        scale = jnp.maximum(0.0, 1.0 - radius_ref[0, b : b + 1, :] / size)
        acc[b] = misfit * scale
        stores[b].start()
    for copy in stores:
        copy.wait()


def forward(tile_list, counts, degrid, dual, observed, radius, image, chips, tile_count):
    _, blocks, depth, entries, pixels = degrid.shape
    channels = dual.shape[-1]
    group = forward_group
    return pl.pallas_call(
        functools.partial(forward_body, chips=chips, tile_count=tile_count, group=group),
        out_shape=jax.ShapeDtypeStruct(dual.shape, jnp.float32),
        in_specs=[hbm_spec] * 5 + [vmem_spec] + [any_spec] * len(image),
        out_specs=hbm_spec,
        scratch_shapes=[
            pltpu.SMEM(tile_list.shape, jnp.int32),
            pltpu.SMEM(counts.shape, jnp.int32),
            pltpu.VMEM((blocks, entries, channels), jnp.float32),
            pltpu.VMEM((blocks, entries, channels), jnp.bfloat16),
            pltpu.VMEM((2 * chips * tile_count + 1, pixels, channels), jnp.bfloat16),
            pltpu.VMEM((blocks, entries, channels), jnp.float32),
            pltpu.VMEM((blocks, depth, entries, pixels), jnp.bfloat16),
            pltpu.SemaphoreType.DMA((blocks, depth // group)),
            pltpu.SemaphoreType.DMA((2 * chips,)),
            pltpu.SemaphoreType.DMA((2 + blocks,)),
            pltpu.SemaphoreType.DMA((2,)),
        ],
        compiler_params=pltpu.CompilerParams(vmem_limit_bytes=32 * MIB),
        name="forward",
    )(
        *(in_hbm(value) for value in (tile_list, counts, degrid, dual, observed)),
        radius,
        *image,
    )


def plus(*values):
    total = values[0].astype(jnp.float32)
    for value in values[1:]:
        total = total + value.astype(jnp.float32)
    return total.astype(jnp.bfloat16)


def to_owners(evens, odds, chips):
    even_far, even_mid, _ = evens
    half = even_far.shape[0] // 2
    far = swap(odds[0], "facet", 1)
    mid = swap(odds[1], "facet", 1)
    low, high = slice(0, half), slice(half, None)
    if chips == 4:
        via_x = swap(plus(even_far[low], far[low]), "facet", 2)
        via_y = swap(plus(even_far[high], far[high]), "facet", 4)
        x_low = swap(plus(even_mid[0, low], mid[0, low]), "facet", 2)
        y_high = swap(plus(even_mid[1, high], mid[1, high]), "facet", 4)
        own = swap(odds[2], "facet", 1)
        x_high = swap(plus(even_mid[0, high], mid[0, high], via_y), "facet", 2)
        y_low = swap(plus(even_mid[1, low], mid[1, low], via_x), "facet", 4)
        return own, [x_low, y_low], [x_high, y_high]
    own = swap(odds[2], "facet", 1)
    lows, highs = [], []
    for k in range(1, chips):
        pair = (even_far, far) if k == chips - 1 else (even_mid[k - 1], mid[k - 1])
        got = swap(plus(*pair), "facet", 2 * k)
        lows.append(got[low])
        highs.append(got[high])
    return own, lows, highs


def from_owners(tiles, chips):
    reached = [tiles]
    for k in range(1, chips):
        reached.append(swap(tiles, "facet", 2 * k))
    image = []
    for k in range(chips):
        image.append(reached[k])
        image.append(swap(reached[k], "facet", 1))
    return image


def per_device(
    sky_image,
    wave_dual,
    rank_dual,
    data_dual,
    observed,
    radius,
    degrid,
    tile_list,
    counts,
    keep_count,
):
    return iteration(
        sky_image,
        wave_dual,
        rank_dual,
        data_dual,
        observed,
        radius,
        degrid,
        tile_list,
        counts.T,
        keep_count,
    )


def iteration(
    sky_image,
    wave_dual,
    rank_dual,
    data_dual,
    observed,
    radius,
    degrid,
    tile_list,
    counts,
    keep_count,
):
    height, columns, _ = sky_image.shape
    facets = lax.axis_size("facet")
    chips = facets // 2
    tile_count = height // TR * (columns // TC)

    even_column = lax.rem(lax.axis_index("facet"), 2) == 0
    even_row = lax.rem(lax.axis_index("dp"), 2) == 0
    tile_list, even_column, even_row = lax.optimization_barrier((tile_list, even_column, even_row))
    sides = (("facet", 1, even_column), ("dp", 0, even_row))
    sums = adjoint(tile_list, counts, data_dual, degrid, chips, tile_count)
    mate_own, low, high = to_owners(sums[:3], sums[3:], chips)

    wave_halo = padded_2(wave_dual, sides, 2)
    rest = synthesis(wave_halo, height, columns) + rank_dual
    sky_next, extrap, tiles = primal(sky_image, rest, sums[2], mate_own, low, high)

    image = from_owners(tiles, chips)
    packed = gram_of(extrap, rank_dual)
    bar_halo = padded_2(extrap, sides, 2)
    wave_next = jnp.clip(
        wave_dual + step_wave * analysis(bar_halo, height, columns), -wave_bound, wave_bound
    )
    stride = 1
    got = swap(packed, "dp", 1)
    while 2 * stride < lax.axis_size("dp"):
        stride = 2 * stride
        packed = packed + got
        got = swap(packed, "dp", stride)
    rank_next = rank_update(keep_count, [packed, got], extrap, rank_dual)
    data_next = forward(
        tile_list, counts, degrid, data_dual, observed, radius, image, chips, tile_count
    )
    return (sky_next, wave_next, rank_next, data_next)


def solution(mesh):
    return jax.shard_map(
        per_device,
        mesh=mesh,
        in_specs=(
            P("dp", "facet", None),
            P("dp", "facet", None),
            P("dp", "facet", None),
            P("facet", "dp", None, None),
            P("facet", "dp", None, None),
            P("facet", "dp", None),
            P("facet", "dp", None, None, None),
            P(None, "dp", None),
            P(None, "dp"),
            P("facet"),
        ),
        out_specs=(
            P("dp", "facet", None),
            P("dp", "facet", None),
            P("dp", "facet", None),
            P("facet", "dp", None, None),
        ),
        check_vma=False,
    )
```

```python
import functools

import jax
import jax.numpy as jnp
from jax import lax
from jax.experimental import pallas as pl
from jax.experimental.pallas import tpu as pltpu
from jax.sharding import PartitionSpec as P


TR = 8
TC = 16
MIB = 1 << 20


wavelet_taps = (-0.12940952255126037, -0.2241438680420134, 0.8365163037378079, -0.48296291314453416)
step_primal = 0.5
step_wave = 0.5
wave_bound = 1.0
step_rank = 0.5

any_spec = pl.BlockSpec(memory_space=pl.ANY)
smem_spec = pl.BlockSpec(memory_space=pltpu.SMEM)
hbm_spec = pl.BlockSpec(memory_space=pltpu.HBM)
vmem_spec = pl.BlockSpec(memory_space=pltpu.VMEM)
adjoint_group = 8
forward_group = 8
forward_limit = 32


def in_hbm(value):
    return pltpu.with_memory_space_constraint(value, pltpu.HBM)


def swap(value, axis, mask):
    count = lax.axis_size(axis)
    return lax.ppermute(value, axis, [(i, i ^ mask) for i in range(count)])


def padded_2(block, sides, width):
    for axis, dim, even in sides:
        count = lax.axis_size(axis)
        outer = [(i, i + 1) for i in range(1, count - 1, 2)]
        outer = outer + [(target, source) for source, target in outer]
        first = lax.slice_in_dim(block, 0, width, axis=dim)
        last = lax.slice_in_dim(block, block.shape[dim] - width, None, axis=dim)
        inward = jnp.where(even, last, first)
        outward = jnp.where(even, first, last)
        inside = swap(inward, axis, 1)
        outside = lax.ppermute(outward, axis, outer)
        low = jnp.where(even, outside, inside)
        high = jnp.where(even, inside, outside)
        block = jnp.concatenate([low, block, high], axis=dim)
    return block


def analysis(padded, height, columns):
    across = sum(
        (
            wavelet_taps[offset] * padded[offset + 1 : offset + 1 + height, :, :]
            for offset in range(4)
        )
    )
    return sum(
        (
            wavelet_taps[offset] * across[:, offset + 1 : offset + 1 + columns, :]
            for offset in range(4)
        )
    )


def synthesis(padded, height, columns):
    across = sum(
        (
            wavelet_taps[offset] * padded[3 - offset : 3 - offset + height, :, :]
            for offset in range(4)
        )
    )
    return sum(
        (
            wavelet_taps[offset] * across[:, 3 - offset : 3 - offset + columns, :]
            for offset in range(4)
        )
    )


def slot_chunks(degrid_hbm, buf, sems, group):
    blocks, depth = degrid_hbm.shape[1:3]
    return [
        [
            pltpu.make_async_copy(
                degrid_hbm.at[0, b, pl.ds(c * group, group)],
                buf.at[b, pl.ds(c * group, group)],
                sems.at[b, c],
            )
            for c in range(depth // group)
        ]
        for b in range(blocks)
    ]


def relative_tile(tiles, me, block, slot, count, tile_count, dummy):
    tile = tiles[me, block, jnp.minimum(slot, count - 1)]
    source = lax.div(tile, tile_count)
    place = lax.bitwise_xor(source, me) * tile_count + (tile - source * tile_count)
    return jnp.where(slot < count, place, dummy)


def adjoint_body(
    tiles_hbm, counts_hbm, dual_hbm, degrid_hbm,
    even_far_ref, even_mid_ref, even_own_ref, odd_far_ref, odd_mid_ref, odd_own_ref,
    tiles, counts, dual, turned, acc, buf, sems, dual_sems, list_sems,
    *, chips, tile_count, group,
):
    blocks, depth = degrid_hbm.shape[1:3]
    pixels = degrid_hbm.shape[4]
    me = lax.axis_index("facet")
    chunks = slot_chunks(degrid_hbm, buf, sems, group)
    lists = [
        pltpu.make_async_copy(counts_hbm, counts, list_sems.at[0]),
        pltpu.make_async_copy(tiles_hbm, tiles, list_sems.at[1]),
    ]
    duals = [
        pltpu.make_async_copy(dual_hbm.at[0, b], dual.at[b], dual_sems.at[b]) for b in range(blocks)
    ]
    for copy in lists:
        copy.start()
    for b in range(blocks):
        duals[b].start()
        chunks[b][0].start()
    acc[...] = jnp.zeros_like(acc)
    for copy in lists:
        copy.wait()
    for b in range(blocks):
        for c in range(1, depth // group):
            @pl.when(c * group < counts[b, me])
            def _():
                chunks[b][c].start()
    live = 2 * chips * tile_count
    for b in range(blocks):
        duals[b].wait()
        turned[b] = dual[b].astype(jnp.bfloat16).T
        for c in range(depth // group):
            @pl.when(c * group < counts[b, me])
            def _():
                chunks[b][c].wait()
                right = jnp.concatenate([buf[b, c * group + j] for j in range(group)], axis=1)
                result = jnp.dot(turned[b], right, preferred_element_type=jnp.float32)
                result = result.astype(jnp.bfloat16).astype(jnp.float32)
                for j in range(group):
                    name = relative_tile(
                        tiles, me, b, c * group + j, counts[b, me], tile_count, live
                    )
                    acc[name] = acc[name] + result[:, j * pixels : (j + 1) * pixels]

    for k in range(chips):
        first = 2 * k * tile_count
        even = acc[first : first + tile_count].astype(jnp.bfloat16)
        odd = acc[first + tile_count : first + 2 * tile_count].astype(jnp.bfloat16)
        if k == chips - 1:
            even_far_ref[...] = even
            odd_far_ref[...] = odd
        elif k:
            even_mid_ref[k - 1] = even
            odd_mid_ref[k - 1] = odd
        else:
            even_own_ref[...] = even
            odd_own_ref[...] = odd


def adjoint(tile_list, counts, dual, degrid, chips, tile_count):
    _, blocks, depth, entries, pixels = degrid.shape
    channels = dual.shape[-1]
    group = adjoint_group

    def tiles_of(*lead):
        return jax.ShapeDtypeStruct(lead + (tile_count, channels, pixels), jnp.bfloat16)

    return pl.pallas_call(
        functools.partial(adjoint_body, chips=chips, tile_count=tile_count, group=group),
        out_shape=[tiles_of(), tiles_of(chips - 2), tiles_of()] * 2,
        in_specs=[hbm_spec] * 4,
        out_specs=[vmem_spec] * 6,
        scratch_shapes=[
            pltpu.SMEM(tile_list.shape, jnp.int32),
            pltpu.SMEM(counts.shape, jnp.int32),
            pltpu.VMEM((blocks, entries, channels), jnp.float32),
            pltpu.VMEM((blocks, channels, entries), jnp.bfloat16),
            pltpu.VMEM((2 * chips * tile_count + 1, channels, pixels), jnp.float32),
            pltpu.VMEM((blocks, depth, entries, pixels), jnp.bfloat16),
            pltpu.SemaphoreType.DMA((blocks, depth // group)),
            pltpu.SemaphoreType.DMA((blocks,)),
            pltpu.SemaphoreType.DMA((2,)),
        ],
        compiler_params=pltpu.CompilerParams(vmem_limit_bytes=(30 if chips == 4 else 50) * MIB),
        name="adjoint",
    )(*(in_hbm(value) for value in (tile_list, counts, dual, degrid)))


def primal_body(*refs, parts):
    sky_ref, base_ref, rest_ref, own_ref, mate_ref = refs[:5]
    halves = (refs[5 : 5 + parts], refs[5 + parts : 5 + 2 * parts])
    next_ref, extrap_ref, tiles_ref = refs[5 + 2 * parts :]
    _, columns, channels = sky_ref.shape
    across = columns // TC
    half = tiles_ref.shape[0] // 2
    for h in range(2):
        for t in range(half):
            tile = h * half + t
            total = own_ref[tile].astype(jnp.float32) + mate_ref[tile].astype(jnp.float32)
            for part in halves[h]:
                total = total + part[t].astype(jnp.float32)
            back = total.T.reshape(TR, TC, channels)
            rows = pl.ds(tile // across * TR, TR)
            cols = pl.ds(tile % across * TC, TC)
            sky = sky_ref[rows, cols, :]
            new = jnp.maximum(
                base_ref[rows, cols, :] - step_primal * (back + rest_ref[rows, cols, :]), 0.0
            )
            extrap = 2.0 * new - sky
            next_ref[rows, cols, :] = new
            extrap_ref[rows, cols, :] = extrap
            tiles_ref[tile] = extrap.reshape(TR * TC, channels).astype(jnp.bfloat16)


def primal(sky, base, rest, own, mate, low, high):
    whole = jax.ShapeDtypeStruct(sky.shape, jnp.float32)
    tiles = jax.ShapeDtypeStruct((own.shape[0], own.shape[2], own.shape[1]), jnp.bfloat16)
    return pl.pallas_call(
        functools.partial(primal_body, parts=len(low)),
        out_shape=[whole, whole, tiles],
        in_specs=[vmem_spec] * (5 + len(low) + len(high)),
        out_specs=[vmem_spec] * 3,
        compiler_params=pltpu.CompilerParams(vmem_limit_bytes=16 * MIB),
        name="primal",
    )(sky, base, rest, own, mate, *low, *high)


def gram_body(extrap_ref, rank_ref, packed_ref):
    height, columns, channels = extrap_ref.shape
    half = channels // 2
    mixed = (rank_ref[...] + step_rank * extrap_ref[...]).reshape(height * columns, channels)
    gram = lax.dot_general(
        mixed, mixed, (((0,), (0,)), ((), ())),
        precision=lax.Precision.HIGHEST, preferred_element_type=jnp.float32,
    )
    row = lax.broadcasted_iota(jnp.int32, (half, half), 0)
    col = lax.broadcasted_iota(jnp.int32, (half, half), 1)
    corner = gram[half:, half:]
    packed_ref[0:half] = jnp.where(col >= row, gram[:half, :half], corner)
    packed_ref[half:channels] = gram[:half, half:]
    packed_ref[channels:] = jnp.broadcast_to(
        jnp.sum(jnp.where(col == row, corner, 0.0), axis=0, keepdims=True), (8, half)
    )


def gram_of(extrap, rank_dual):
    channels = extrap.shape[2]
    return pl.pallas_call(
        gram_body,
        out_shape=jax.ShapeDtypeStruct((channels + 8, channels // 2), jnp.float32),
        in_specs=[vmem_spec, vmem_spec],
        out_specs=vmem_spec,
        compiler_params=pltpu.CompilerParams(vmem_limit_bytes=16 * MIB),
        name="gram",
    )(extrap, rank_dual)


def split(value):
    high = value.astype(jnp.bfloat16)
    return high, (value - high.astype(jnp.float32)).astype(jnp.bfloat16)


def dot_fine(left, right):
    a, b = split(left)
    c, d = split(right)
    return jnp.dot(
        jnp.concatenate([a, a, b], axis=1),
        jnp.concatenate([c, d, c], axis=0),
        preferred_element_type=jnp.float32,
    )


def dot_full(left, right):
    return jnp.dot(
        left, right, precision=lax.Precision.HIGHEST, preferred_element_type=jnp.float32
    )


def dot_quick(left, right):
    return jnp.dot(
        left.astype(jnp.bfloat16), right.astype(jnp.bfloat16), preferred_element_type=jnp.float32
    )


def rank_body(keep_ref, *refs, parts):
    packed_refs = refs[:parts]
    extrap_hbm, rank_hbm, out_ref, extrap_buf, rank_buf, sems = refs[parts:]
    loads = [
        pltpu.make_async_copy(extrap_hbm, extrap_buf, sems.at[0]),
        pltpu.make_async_copy(rank_hbm, rank_buf, sems.at[1]),
    ]
    for load in loads:
        load.start()
    height, columns, channels = extrap_buf.shape
    half = channels // 2
    packed = packed_refs[0][...]
    for ref in packed_refs[1:]:
        packed = packed + ref[...]
    row = lax.broadcasted_iota(jnp.int32, (half, half), 0)
    col = lax.broadcasted_iota(jnp.int32, (half, half), 1)
    mix = packed[:half]
    upper = jnp.where(col > row, mix, 0.0)
    lower = jnp.where(col < row, mix, 0.0)
    first = jnp.where(col >= row, mix, 0.0) + upper.T
    tail = packed[channels : channels + 1]
    last = lower + lower.T + jnp.where(col == row, jnp.broadcast_to(tail, (half, half)), 0.0)
    cross = packed[half:channels]
    gram = jnp.concatenate(
        [jnp.concatenate([first, cross], axis=1), jnp.concatenate([cross.T, last], axis=1)], axis=0
    )
    wide_row = lax.broadcasted_iota(jnp.int32, (channels, channels), 0)
    wide_col = lax.broadcasted_iota(jnp.int32, (channels, channels), 1)
    eye = jnp.where(wide_row == wide_col, 1.0, 0.0).astype(jnp.float32)
    keep = jnp.full((1, 1), keep_ref[0], jnp.int32).astype(jnp.float32)
    trace = jnp.sum(jnp.sum(gram * eye, axis=0, keepdims=True), axis=1, keepdims=True)
    level = (trace + 1e-06) / keep
    system = gram / level + eye
    scale = 2.0 / (2.0 + keep)
    error = eye - scale * system
    inverse = scale * (eye + error)
    error = dot_quick(error, error)
    for step in range(6):
        if step < 5:
            both = dot_quick(jnp.concatenate([inverse, error], axis=0), error)
            inverse = inverse + both[:channels]
            error = both[channels:]
        else:
            inverse = inverse + dot_quick(inverse, error)
    residual = eye - dot_fine(system, inverse)
    residual = residual + dot_quick(residual, residual)
    inverse = inverse + dot_fine(inverse, residual)
    residual = eye - dot_full(system, inverse)
    inverse = inverse + dot_fine(inverse, residual)
    for load in loads:
        load.wait()
    mixed = (rank_buf[...] + step_rank * extrap_buf[...]).reshape(height * columns, channels)
    out_ref[...] = dot_fine(mixed, inverse).reshape(height, columns, channels)


def rank_update(keep_count, packed, extrap, rank_dual):
    return pl.pallas_call(
        functools.partial(rank_body, parts=len(packed)),
        out_shape=jax.ShapeDtypeStruct(extrap.shape, jnp.float32),
        in_specs=[smem_spec] + [vmem_spec] * len(packed) + [any_spec, any_spec],
        out_specs=vmem_spec,
        scratch_shapes=[
            pltpu.VMEM(extrap.shape, jnp.float32),
            pltpu.VMEM(extrap.shape, jnp.float32),
            pltpu.SemaphoreType.DMA((2,)),
        ],
        compiler_params=pltpu.CompilerParams(vmem_limit_bytes=12 * MIB),
        name="rank",
    )(keep_count, *packed, extrap, rank_dual)


def forward_body(
    tiles, counts, degrid_ref, dual_hbm, seen_hbm, radius_ref, *refs, chips, tile_count, group
):
    image_refs, out_hbm = refs[:-8], refs[-8]
    image, acc, dual, seen, image_sems, load_sems, store_sems = refs[-7:]
    blocks, depth, _, _ = degrid_ref.shape[1:5]
    me = lax.axis_index("facet")
    images = []
    live = 0
    for i, ref in enumerate(image_refs):
        size = ref.shape[0]
        images.append(
            pltpu.make_async_copy(ref, image.at[pl.ds(live, size)], image_sems.at[i])
        )
        live += size
    stores = [
        pltpu.make_async_copy(acc.at[b], out_hbm.at[0, b], store_sems.at[b]) for b in range(blocks)
    ]
    loads = [
        pltpu.make_async_copy(dual_hbm.at[0], dual, load_sems.at[0]),
        pltpu.make_async_copy(seen_hbm.at[0], seen, load_sems.at[1]),
    ]
    for copy in images + loads:
        copy.start()
    image[live] = jnp.zeros_like(image[live])
    for copy in images:
        copy.wait()
    for b in range(blocks):
        for c in range(depth // group):
            @pl.when(c * group < counts[b, me])
            def _():
                names = [
                    relative_tile(tiles, me, b, c * group + j, counts[b, me], tile_count, live)
                    for j in range(group)
                ]
                left = jnp.concatenate(
                    [degrid_ref[0, b, c * group + j] for j in range(group)], axis=1
                )
                right = jnp.concatenate([image[name] for name in names], axis=0)
                product = jnp.dot(left, right, preferred_element_type=jnp.float32)
                acc[b] = acc[b] + product if c else product

        if b == 0:
            for copy in loads:
                copy.wait()
        misfit = acc[b] + (dual[b] - seen[b].astype(jnp.float32))
        size = jnp.sqrt(jnp.sum(misfit * misfit, axis=0, keepdims=True) + 1e-06)
        scale = jnp.maximum(0.0, 1.0 - radius_ref[0, b : b + 1, :] / size)
        acc[b] = misfit * scale
        stores[b].start()
    for copy in stores:
        copy.wait()


def forward(tile_list, counts, degrid, dual, observed, radius, image, chips, tile_count):
    _, blocks, _, entries, pixels = degrid.shape
    channels = dual.shape[-1]
    group = forward_group
    return pl.pallas_call(
        functools.partial(forward_body, chips=chips, tile_count=tile_count, group=group),
        out_shape=jax.ShapeDtypeStruct(dual.shape, jnp.float32),
        in_specs=[smem_spec, smem_spec, vmem_spec, hbm_spec, hbm_spec, vmem_spec]
        + [any_spec] * len(image),
        out_specs=hbm_spec,
        scratch_shapes=[
            pltpu.VMEM((2 * chips * tile_count + 1, pixels, channels), jnp.bfloat16),
            pltpu.VMEM((blocks, entries, channels), jnp.float32),
            pltpu.VMEM((blocks, entries, channels), jnp.float32),
            pltpu.VMEM((blocks, entries, channels), jnp.bfloat16),
            pltpu.SemaphoreType.DMA((len(image),)),
            pltpu.SemaphoreType.DMA((2,)),
            pltpu.SemaphoreType.DMA((blocks,)),
        ],
        compiler_params=pltpu.CompilerParams(vmem_limit_bytes=forward_limit * MIB),
        name="forward",
    )(tile_list, counts, degrid, in_hbm(dual), in_hbm(observed), radius, *image)


def plus(*values):
    total = values[0].astype(jnp.float32)
    for value in values[1:]:
        total = total + value.astype(jnp.float32)
    return total.astype(jnp.bfloat16)


def to_owners(evens, odds, chips):
    even_far, even_mid, _ = evens
    half = even_far.shape[0] // 2
    far = swap(odds[0], "facet", 1)
    mid = swap(odds[1], "facet", 1)
    low, high = slice(0, half), slice(half, None)
    if chips == 4:
        via_x = swap(plus(even_far[low], far[low]), "facet", 2)
        via_y = swap(plus(even_far[high], far[high]), "facet", 4)
        x_low = swap(plus(even_mid[0, low], mid[0, low]), "facet", 2)
        y_high = swap(plus(even_mid[1, high], mid[1, high]), "facet", 4)
        own = swap(odds[2], "facet", 1)
        x_high = swap(plus(even_mid[0, high], mid[0, high], via_y), "facet", 2)
        y_low = swap(plus(even_mid[1, low], mid[1, low], via_x), "facet", 4)
        return own, [x_low, y_low], [x_high, y_high]
    own = swap(odds[2], "facet", 1)
    lows, highs = [], []
    for k in range(1, chips):
        pair = (even_far, far) if k == chips - 1 else (even_mid[k - 1], mid[k - 1])
        got = swap(plus(*pair), "facet", 2 * k)
        lows.append(got[low])
        highs.append(got[high])
    return own, lows, highs


def from_owners(tiles, chips):
    reached = [[tiles]]
    if chips == 4:
        half = tiles.shape[0] // 2
        x, y = swap(tiles, "facet", 2), swap(tiles, "facet", 4)
        low = swap(x[:half], "facet", 4)
        high = swap(y[half:], "facet", 2)
        reached += [[x], [y], [low, high]]
    else:
        reached += [[swap(tiles, "facet", 2 * k)] for k in range(1, chips)]
    image = []
    for parts in reached:
        image += parts
        image += [swap(part, "facet", 1) for part in parts]
    return image


def per_device(
    sky_image,
    wave_dual,
    rank_dual,
    data_dual,
    observed,
    radius,
    degrid,
    tile_list,
    counts,
    keep_count,
):
    return iteration(
        sky_image,
        wave_dual,
        rank_dual,
        data_dual,
        observed,
        radius,
        degrid,
        tile_list,
        counts.T,
        keep_count,
    )


def iteration(
    sky_image,
    wave_dual,
    rank_dual,
    data_dual,
    observed,
    radius,
    degrid,
    tile_list,
    counts,
    keep_count,
):
    height, columns, _ = sky_image.shape
    facets = lax.axis_size("facet")
    chips = facets // 2
    tile_count = height // TR * (columns // TC)

    even_column = lax.rem(lax.axis_index("facet"), 2) == 0
    even_row = lax.rem(lax.axis_index("dp"), 2) == 0
    tile_list, even_column, even_row = lax.optimization_barrier((tile_list, even_column, even_row))
    sides = (("facet", 1, even_column), ("dp", 0, even_row))
    sums = adjoint(tile_list, counts, data_dual, degrid, chips, tile_count)
    mate_own, low, high = to_owners(sums[:3], sums[3:], chips)

    wave_halo = padded_2(wave_dual, sides, 2)
    base = sky_image - step_primal * rank_dual
    rest = synthesis(wave_halo, height, columns)
    sky_next, extrap, tiles = primal(sky_image, base, rest, sums[2], mate_own, low, high)

    image = from_owners(tiles, chips)
    packed = gram_of(extrap, rank_dual)
    bar_halo = padded_2(extrap, sides, 2)
    wave_next = jnp.clip(
        wave_dual + step_wave * analysis(bar_halo, height, columns), -wave_bound, wave_bound
    )
    stride = 1
    got = swap(packed, "dp", 1)
    while 2 * stride < lax.axis_size("dp"):
        stride = 2 * stride
        packed = packed + got
        got = swap(packed, "dp", stride)
    rank_next = rank_update(keep_count, [packed, got], extrap, rank_dual)
    data_next = forward(
        tile_list, counts, degrid, data_dual, observed, radius, image, chips, tile_count
    )
    return (sky_next, wave_next, rank_next, data_next)


def solution(mesh):
    return jax.shard_map(
        per_device,
        mesh=mesh,
        in_specs=(
            P("dp", "facet", None),
            P("dp", "facet", None),
            P("dp", "facet", None),
            P("facet", "dp", None, None),
            P("facet", "dp", None, None),
            P("facet", "dp", None),
            P("facet", "dp", None, None, None),
            P(None, "dp", None),
            P(None, "dp"),
            P("facet"),
        ),
        out_specs=(
            P("dp", "facet", None),
            P("dp", "facet", None),
            P("dp", "facet", None),
            P("facet", "dp", None, None),
        ),
        check_vma=False,
    )
```

```python
import functools

import jax
import jax.numpy as jnp
from jax import lax
from jax.experimental import pallas as pl
from jax.experimental.pallas import tpu as pltpu
from jax.sharding import PartitionSpec as P


TR = 8
TC = 16
MIB = 1 << 20


wavelet_taps = (-0.12940952255126037, -0.2241438680420134, 0.8365163037378079, -0.48296291314453416)
step_primal = 0.5
step_wave = 0.5
wave_bound = 1.0
step_rank = 0.5

any_spec = pl.BlockSpec(memory_space=pl.ANY)
smem_spec = pl.BlockSpec(memory_space=pltpu.SMEM)
hbm_spec = pl.BlockSpec(memory_space=pltpu.HBM)
vmem_spec = pl.BlockSpec(memory_space=pltpu.VMEM)
adjoint_group = 8
forward_group = 8
forward_limit = 32


def in_hbm(value):
    return pltpu.with_memory_space_constraint(value, pltpu.HBM)


def swap(value, axis, mask):
    count = lax.axis_size(axis)
    return lax.ppermute(value, axis, [(i, i ^ mask) for i in range(count)])


def padded_2(block, sides, width):
    for axis, dim, even in sides:
        count = lax.axis_size(axis)
        outer = [(i, i + 1) for i in range(1, count - 1, 2)]
        outer = outer + [(target, source) for source, target in outer]
        first = lax.slice_in_dim(block, 0, width, axis=dim)
        last = lax.slice_in_dim(block, block.shape[dim] - width, None, axis=dim)
        inward = jnp.where(even, last, first)
        outward = jnp.where(even, first, last)
        inside = swap(inward, axis, 1)
        outside = lax.ppermute(outward, axis, outer)
        low = jnp.where(even, outside, inside)
        high = jnp.where(even, inside, outside)
        block = jnp.concatenate([low, block, high], axis=dim)
    return block


def analysis(padded, height, columns):
    across = sum(
        (
            wavelet_taps[offset] * padded[offset + 1 : offset + 1 + height, :, :]
            for offset in range(4)
        )
    )
    return sum(
        (
            wavelet_taps[offset] * across[:, offset + 1 : offset + 1 + columns, :]
            for offset in range(4)
        )
    )


def synthesis(padded, height, columns):
    across = sum(
        (
            wavelet_taps[offset] * padded[3 - offset : 3 - offset + height, :, :]
            for offset in range(4)
        )
    )
    return sum(
        (
            wavelet_taps[offset] * across[:, 3 - offset : 3 - offset + columns, :]
            for offset in range(4)
        )
    )


def slot_chunks(degrid_hbm, buf, sems, group):
    blocks, depth = degrid_hbm.shape[1:3]
    return [
        [
            pltpu.make_async_copy(
                degrid_hbm.at[0, b, pl.ds(c * group, group)],
                buf.at[b, pl.ds(c * group, group)],
                sems.at[b, c],
            )
            for c in range(depth // group)
        ]
        for b in range(blocks)
    ]


def relative_tile(tiles, me, block, slot, count, tile_count, dummy):
    tile = tiles[me, block, jnp.minimum(slot, count - 1)]
    source = lax.div(tile, tile_count)
    place = lax.bitwise_xor(source, me) * tile_count + (tile - source * tile_count)
    return jnp.where(slot < count, place, dummy)


def adjoint_body(
    tiles_hbm, counts_hbm, dual_hbm, degrid_hbm,
    even_far_ref, even_mid_ref, even_own_ref, odd_far_ref, odd_mid_ref, odd_own_ref,
    tiles, counts, dual, turned, acc, buf, sems, dual_sems, list_sems,
    *, chips, tile_count, group,
):
    blocks, depth = degrid_hbm.shape[1:3]
    pixels = degrid_hbm.shape[4]
    me = lax.axis_index("facet")
    chunks = slot_chunks(degrid_hbm, buf, sems, group)
    lists = [
        pltpu.make_async_copy(counts_hbm, counts, list_sems.at[0]),
        pltpu.make_async_copy(tiles_hbm, tiles, list_sems.at[1]),
    ]
    duals = [
        pltpu.make_async_copy(dual_hbm.at[0, b], dual.at[b], dual_sems.at[b]) for b in range(blocks)
    ]
    for copy in lists:
        copy.start()
    for b in range(blocks):
        duals[b].start()
        chunks[b][0].start()
    acc[...] = jnp.zeros_like(acc)
    for copy in lists:
        copy.wait()
    for b in range(blocks):
        for c in range(1, depth // group):
            @pl.when(c * group < counts[b, me])
            def _():
                chunks[b][c].start()
    live = 2 * chips * tile_count
    for b in range(blocks):
        duals[b].wait()
        turned[b] = dual[b].astype(jnp.bfloat16).T
        for c in range(depth // group):
            @pl.when(c * group < counts[b, me])
            def _():
                chunks[b][c].wait()
                right = jnp.concatenate([buf[b, c * group + j] for j in range(group)], axis=1)
                result = jnp.dot(turned[b], right, preferred_element_type=jnp.float32)
                result = result.astype(jnp.bfloat16).astype(jnp.float32)
                for j in range(group):
                    name = relative_tile(
                        tiles, me, b, c * group + j, counts[b, me], tile_count, live
                    )
                    acc[name] = acc[name] + result[:, j * pixels : (j + 1) * pixels]

    for k in range(chips):
        first = 2 * k * tile_count
        even = acc[first : first + tile_count].astype(jnp.bfloat16)
        odd = acc[first + tile_count : first + 2 * tile_count].astype(jnp.bfloat16)
        if k == chips - 1:
            even_far_ref[...] = even
            odd_far_ref[...] = odd
        elif k:
            even_mid_ref[k - 1] = even
            odd_mid_ref[k - 1] = odd
        else:
            even_own_ref[...] = even
            odd_own_ref[...] = odd


def adjoint(tile_list, counts, dual, degrid, chips, tile_count):
    _, blocks, depth, entries, pixels = degrid.shape
    channels = dual.shape[-1]
    group = adjoint_group

    def tiles_of(*lead):
        return jax.ShapeDtypeStruct(lead + (tile_count, channels, pixels), jnp.bfloat16)

    return pl.pallas_call(
        functools.partial(adjoint_body, chips=chips, tile_count=tile_count, group=group),
        out_shape=[tiles_of(), tiles_of(chips - 2), tiles_of()] * 2,
        in_specs=[hbm_spec] * 4,
        out_specs=[vmem_spec] * 6,
        scratch_shapes=[
            pltpu.SMEM(tile_list.shape, jnp.int32),
            pltpu.SMEM(counts.shape, jnp.int32),
            pltpu.VMEM((blocks, entries, channels), jnp.float32),
            pltpu.VMEM((blocks, channels, entries), jnp.bfloat16),
            pltpu.VMEM((2 * chips * tile_count + 1, channels, pixels), jnp.float32),
            pltpu.VMEM((blocks, depth, entries, pixels), jnp.bfloat16),
            pltpu.SemaphoreType.DMA((blocks, depth // group)),
            pltpu.SemaphoreType.DMA((blocks,)),
            pltpu.SemaphoreType.DMA((2,)),
        ],
        compiler_params=pltpu.CompilerParams(vmem_limit_bytes=(30 if chips == 4 else 50) * MIB),
        name="adjoint",
    )(*(in_hbm(value) for value in (tile_list, counts, dual, degrid)))


def primal_body(*refs, parts):
    sky_ref, base_ref, rest_ref, own_ref, mate_ref = refs[:5]
    halves = (refs[5 : 5 + parts], refs[5 + parts : 5 + 2 * parts])
    extrap_ref, tiles_ref = refs[5 + 2 * parts :]
    _, columns, channels = sky_ref.shape
    across = columns // TC
    half = tiles_ref.shape[0] // 2
    for h in range(2):
        for t in range(half):
            tile = h * half + t
            total = own_ref[tile].astype(jnp.float32) + mate_ref[tile].astype(jnp.float32)
            for part in halves[h]:
                total = total + part[t].astype(jnp.float32)
            back = total.T.reshape(TR, TC, channels)
            rows = pl.ds(tile // across * TR, TR)
            cols = pl.ds(tile % across * TC, TC)
            sky = sky_ref[rows, cols, :]
            new = jnp.maximum(
                base_ref[rows, cols, :] - step_primal * (back + rest_ref[rows, cols, :]), 0.0
            )
            extrap = 2.0 * new - sky
            extrap_ref[rows, cols, :] = extrap
            tiles_ref[tile] = extrap.reshape(TR * TC, channels).astype(jnp.bfloat16)


def primal(sky, base, rest, own, mate, low, high):
    whole = jax.ShapeDtypeStruct(sky.shape, jnp.float32)
    tiles = jax.ShapeDtypeStruct((own.shape[0], own.shape[2], own.shape[1]), jnp.bfloat16)
    return pl.pallas_call(
        functools.partial(primal_body, parts=len(low)),
        out_shape=[whole, tiles],
        in_specs=[vmem_spec] * (5 + len(low) + len(high)),
        out_specs=[vmem_spec] * 2,
        compiler_params=pltpu.CompilerParams(vmem_limit_bytes=16 * MIB),
        name="primal",
    )(sky, base, rest, own, mate, *low, *high)


def gram_body(extrap_ref, rank_ref, packed_ref):
    height, columns, channels = extrap_ref.shape
    half = channels // 2
    mixed = (rank_ref[...] + step_rank * extrap_ref[...]).reshape(height * columns, channels)
    gram = lax.dot_general(
        mixed, mixed, (((0,), (0,)), ((), ())),
        precision=lax.Precision.HIGHEST, preferred_element_type=jnp.float32,
    )
    row = lax.broadcasted_iota(jnp.int32, (half, half), 0)
    col = lax.broadcasted_iota(jnp.int32, (half, half), 1)
    corner = gram[half:, half:]
    packed_ref[0:half] = jnp.where(col >= row, gram[:half, :half], corner)
    packed_ref[half:channels] = gram[:half, half:]
    packed_ref[channels:] = jnp.broadcast_to(
        jnp.sum(jnp.where(col == row, corner, 0.0), axis=0, keepdims=True), (8, half)
    )


def gram_of(extrap, rank_dual):
    channels = extrap.shape[2]
    return pl.pallas_call(
        gram_body,
        out_shape=jax.ShapeDtypeStruct((channels + 8, channels // 2), jnp.float32),
        in_specs=[vmem_spec, vmem_spec],
        out_specs=vmem_spec,
        compiler_params=pltpu.CompilerParams(vmem_limit_bytes=16 * MIB),
        name="gram",
    )(extrap, rank_dual)


def split(value):
    high = value.astype(jnp.bfloat16)
    return high, (value - high.astype(jnp.float32)).astype(jnp.bfloat16)


def dot_fine(left, right):
    a, b = split(left)
    c, d = split(right)
    return jnp.dot(
        jnp.concatenate([a, a, b], axis=1),
        jnp.concatenate([c, d, c], axis=0),
        preferred_element_type=jnp.float32,
    )


def dot_full(left, right):
    return jnp.dot(
        left, right, precision=lax.Precision.HIGHEST, preferred_element_type=jnp.float32
    )


def dot_quick(left, right):
    return jnp.dot(
        left.astype(jnp.bfloat16), right.astype(jnp.bfloat16), preferred_element_type=jnp.float32
    )


def rank_body(keep_ref, *refs, parts):
    packed_refs = refs[:parts]
    extrap_hbm, rank_hbm, out_hbm, extrap_buf, rank_buf, out_buf, sems = refs[parts:]
    loads = [
        pltpu.make_async_copy(extrap_hbm, extrap_buf, sems.at[0]),
        pltpu.make_async_copy(rank_hbm, rank_buf, sems.at[1]),
    ]
    for load in loads:
        load.start()
    height, columns, channels = extrap_buf.shape
    half = channels // 2
    packed = packed_refs[0][...]
    for ref in packed_refs[1:]:
        packed = packed + ref[...]
    row = lax.broadcasted_iota(jnp.int32, (half, half), 0)
    col = lax.broadcasted_iota(jnp.int32, (half, half), 1)
    mix = packed[:half]
    upper = jnp.where(col > row, mix, 0.0)
    lower = jnp.where(col < row, mix, 0.0)
    first = jnp.where(col >= row, mix, 0.0) + upper.T
    tail = packed[channels : channels + 1]
    last = lower + lower.T + jnp.where(col == row, jnp.broadcast_to(tail, (half, half)), 0.0)
    cross = packed[half:channels]
    gram = jnp.concatenate(
        [jnp.concatenate([first, cross], axis=1), jnp.concatenate([cross.T, last], axis=1)], axis=0
    )
    wide_row = lax.broadcasted_iota(jnp.int32, (channels, channels), 0)
    wide_col = lax.broadcasted_iota(jnp.int32, (channels, channels), 1)
    eye = jnp.where(wide_row == wide_col, 1.0, 0.0).astype(jnp.float32)
    keep = jnp.full((1, 1), keep_ref[0], jnp.int32).astype(jnp.float32)
    trace = jnp.sum(jnp.sum(gram * eye, axis=0, keepdims=True), axis=1, keepdims=True)
    level = (trace + 1e-06) / keep
    system = gram / level + eye
    scale = 2.0 / (2.0 + keep)
    error = eye - scale * system
    inverse = scale * (eye + error)
    error = dot_quick(error, error)
    for step in range(6):
        if step < 5:
            both = dot_quick(jnp.concatenate([inverse, error], axis=0), error)
            inverse = inverse + both[:channels]
            error = both[channels:]
        else:
            inverse = inverse + dot_quick(inverse, error)
    residual = eye - dot_fine(system, inverse)
    residual = residual + dot_quick(residual, residual)
    inverse = inverse + dot_fine(inverse, residual)
    residual = eye - dot_full(system, inverse)
    inverse = inverse + dot_fine(inverse, residual)
    for load in loads:
        load.wait()
    high, low = split(inverse)
    right = jnp.concatenate([high, low, high], axis=0)
    stores = []
    share = height // 4
    for i in range(4):
        rows = pl.ds(i * share, share)
        mixed = (rank_buf[rows] + step_rank * extrap_buf[rows]).reshape(share * columns, channels)
        high, low = split(mixed)
        left = jnp.concatenate([high, high, low], axis=1)
        product = jnp.dot(left, right, preferred_element_type=jnp.float32)
        out_buf[rows] = product.reshape(share, columns, channels)
        stores.append(pltpu.make_async_copy(out_buf.at[rows], out_hbm.at[rows], sems.at[2 + i]))
        stores[i].start()
    for store in stores:
        store.wait()


def rank_update(keep_count, packed, extrap, rank_dual):
    return pl.pallas_call(
        functools.partial(rank_body, parts=len(packed)),
        out_shape=jax.ShapeDtypeStruct(extrap.shape, jnp.float32),
        in_specs=[smem_spec] + [vmem_spec] * len(packed) + [any_spec, any_spec],
        out_specs=hbm_spec,
        scratch_shapes=[
            pltpu.VMEM(extrap.shape, jnp.float32),
            pltpu.VMEM(extrap.shape, jnp.float32),
            pltpu.VMEM(extrap.shape, jnp.float32),
            pltpu.SemaphoreType.DMA((6,)),
        ],
        compiler_params=pltpu.CompilerParams(vmem_limit_bytes=14 * MIB),
        name="rank",
    )(keep_count, *packed, extrap, rank_dual)


def forward_body(
    tiles, counts, degrid_ref, dual_hbm, seen_hbm, radius_ref, *refs, chips, tile_count, group
):
    image_refs, out_hbm = refs[:-8], refs[-8]
    image, acc, dual, seen, image_sems, load_sems, store_sems = refs[-7:]
    blocks, depth, entries, _ = degrid_ref.shape[1:5]
    me = lax.axis_index("facet")
    images = []
    live = 0
    for i, ref in enumerate(image_refs):
        size = ref.shape[0]
        images.append(
            pltpu.make_async_copy(ref, image.at[pl.ds(live, size)], image_sems.at[i])
        )
        live += size
    cut = entries // 4
    stores = [
        [
            pltpu.make_async_copy(
                acc.at[b, pl.ds(i * cut, cut)], out_hbm.at[0, b, pl.ds(i * cut, cut)], store_sems.at[b, i]
            )
            for i in range(4)
        ]
        for b in range(blocks)
    ]
    loads = [
        pltpu.make_async_copy(dual_hbm.at[0], dual, load_sems.at[0]),
        pltpu.make_async_copy(seen_hbm.at[0], seen, load_sems.at[1]),
    ]
    for copy in images + loads:
        copy.start()
    image[live] = jnp.zeros_like(image[live])
    for copy in images:
        copy.wait()
    for b in range(blocks):
        for c in range(depth // group):
            @pl.when(c * group < counts[b, me])
            def _():
                names = [
                    relative_tile(tiles, me, b, c * group + j, counts[b, me], tile_count, live)
                    for j in range(group)
                ]
                left = jnp.concatenate(
                    [degrid_ref[0, b, c * group + j] for j in range(group)], axis=1
                )
                right = jnp.concatenate([image[name] for name in names], axis=0)
                product = jnp.dot(left, right, preferred_element_type=jnp.float32)
                acc[b] = acc[b] + product if c else product

        if b == 0:
            for copy in loads:
                copy.wait()
        misfit = acc[b] + (dual[b] - seen[b].astype(jnp.float32))
        size = jnp.sqrt(jnp.sum(misfit * misfit, axis=0, keepdims=True) + 1e-06)
        scale = jnp.maximum(0.0, 1.0 - radius_ref[0, b : b + 1, :] / size)
        for i in range(4):
            acc[b, i * cut : (i + 1) * cut] = misfit[i * cut : (i + 1) * cut] * scale
            stores[b][i].start()
    for b in range(blocks):
        for copy in stores[b]:
            copy.wait()


def forward(tile_list, counts, degrid, dual, observed, radius, image, chips, tile_count):
    _, blocks, _, entries, pixels = degrid.shape
    channels = dual.shape[-1]
    group = forward_group
    return pl.pallas_call(
        functools.partial(forward_body, chips=chips, tile_count=tile_count, group=group),
        out_shape=jax.ShapeDtypeStruct(dual.shape, jnp.float32),
        in_specs=[smem_spec, smem_spec, vmem_spec, hbm_spec, hbm_spec, vmem_spec]
        + [any_spec] * len(image),
        out_specs=hbm_spec,
        scratch_shapes=[
            pltpu.VMEM((2 * chips * tile_count + 1, pixels, channels), jnp.bfloat16),
            pltpu.VMEM((blocks, entries, channels), jnp.float32),
            pltpu.VMEM((blocks, entries, channels), jnp.float32),
            pltpu.VMEM((blocks, entries, channels), jnp.bfloat16),
            pltpu.SemaphoreType.DMA((len(image),)),
            pltpu.SemaphoreType.DMA((2,)),
            pltpu.SemaphoreType.DMA((blocks, 4)),
        ],
        compiler_params=pltpu.CompilerParams(vmem_limit_bytes=forward_limit * MIB),
        name="forward",
    )(tile_list, counts, degrid, in_hbm(dual), in_hbm(observed), radius, *image)


def plus(*values):
    total = values[0].astype(jnp.float32)
    for value in values[1:]:
        total = total + value.astype(jnp.float32)
    return total.astype(jnp.bfloat16)


def to_owners(evens, odds, chips):
    even_far, even_mid, _ = evens
    half = even_far.shape[0] // 2
    far = swap(odds[0], "facet", 1)
    mid = swap(odds[1], "facet", 1)
    low, high = slice(0, half), slice(half, None)
    if chips == 4:
        via_x = swap(plus(even_far[low], far[low]), "facet", 2)
        via_y = swap(plus(even_far[high], far[high]), "facet", 4)
        x_low = swap(plus(even_mid[0, low], mid[0, low]), "facet", 2)
        y_high = swap(plus(even_mid[1, high], mid[1, high]), "facet", 4)
        own = swap(odds[2], "facet", 1)
        x_high = swap(plus(even_mid[0, high], mid[0, high], via_y), "facet", 2)
        y_low = swap(plus(even_mid[1, low], mid[1, low], via_x), "facet", 4)
        return own, [x_low, y_low], [x_high, y_high]
    own = swap(odds[2], "facet", 1)
    lows, highs = [], []
    for k in range(1, chips):
        pair = (even_far, far) if k == chips - 1 else (even_mid[k - 1], mid[k - 1])
        got = swap(plus(*pair), "facet", 2 * k)
        lows.append(got[low])
        highs.append(got[high])
    return own, lows, highs


def from_owners(tiles, chips):
    reached = [[tiles]]
    if chips == 4:
        half = tiles.shape[0] // 2
        x, y = swap(tiles, "facet", 2), swap(tiles, "facet", 4)
        low = swap(x[:half], "facet", 4)
        high = swap(y[half:], "facet", 2)
        reached += [[x], [y], [low, high]]
    else:
        reached += [[swap(tiles, "facet", 2 * k)] for k in range(1, chips)]
    image = []
    for parts in reached:
        image += parts
        image += [swap(part, "facet", 1) for part in parts]
    return image


def per_device(
    sky_image,
    wave_dual,
    rank_dual,
    data_dual,
    observed,
    radius,
    degrid,
    tile_list,
    counts,
    keep_count,
):
    return iteration(
        sky_image,
        wave_dual,
        rank_dual,
        data_dual,
        observed,
        radius,
        degrid,
        tile_list,
        counts.T,
        keep_count,
    )


def iteration(
    sky_image,
    wave_dual,
    rank_dual,
    data_dual,
    observed,
    radius,
    degrid,
    tile_list,
    counts,
    keep_count,
):
    height, columns, _ = sky_image.shape
    facets = lax.axis_size("facet")
    chips = facets // 2
    tile_count = height // TR * (columns // TC)

    even_column = lax.rem(lax.axis_index("facet"), 2) == 0
    even_row = lax.rem(lax.axis_index("dp"), 2) == 0
    tile_list, even_column, even_row = lax.optimization_barrier((tile_list, even_column, even_row))
    sides = (("facet", 1, even_column), ("dp", 0, even_row))
    sums = adjoint(tile_list, counts, data_dual, degrid, chips, tile_count)
    mate_own, low, high = to_owners(sums[:3], sums[3:], chips)

    wave_halo = padded_2(wave_dual, sides, 2)
    base = sky_image - step_primal * rank_dual
    rest = synthesis(wave_halo, height, columns)
    extrap, tiles = primal(sky_image, base, rest, sums[2], mate_own, low, high)

    sky_next = 0.5 * (extrap + sky_image)

    image = from_owners(tiles, chips)
    packed = gram_of(extrap, rank_dual)
    bar_halo = padded_2(extrap, sides, 2)
    wave_next = jnp.clip(
        wave_dual + step_wave * analysis(bar_halo, height, columns), -wave_bound, wave_bound
    )
    stride = 1
    got = swap(packed, "dp", 1)
    while 2 * stride < lax.axis_size("dp"):
        stride = 2 * stride
        packed = packed + got
        got = swap(packed, "dp", stride)
    rank_next = rank_update(keep_count, [packed, got], extrap, rank_dual)
    data_next = forward(
        tile_list, counts, degrid, data_dual, observed, radius, image, chips, tile_count
    )
    return (sky_next, wave_next, rank_next, data_next)


def solution(mesh):
    return jax.shard_map(
        per_device,
        mesh=mesh,
        in_specs=(
            P("dp", "facet", None),
            P("dp", "facet", None),
            P("dp", "facet", None),
            P("facet", "dp", None, None),
            P("facet", "dp", None, None),
            P("facet", "dp", None),
            P("facet", "dp", None, None, None),
            P(None, "dp", None),
            P(None, "dp"),
            P("facet"),
        ),
        out_specs=(
            P("dp", "facet", None),
            P("dp", "facet", None),
            P("dp", "facet", None),
            P("facet", "dp", None, None),
        ),
        check_vma=False,
    )
```
